32 devices in a mesh: gx: 4 (over y, x), gy: 2 (over core), gz: 4 (over z).
Axes of the slice: x: 2, y: 2, z: 4, core: 2. Of those that a mesh axis runs over, the one named last changes fastest.
Arguments:
- offsets: float32 [3, 8, 4, 8, 128], P(None, 'gx', 'gy', 'gz'), may hold values from 0 to 1
- velocity: float32 [3, 8, 4, 8, 128], P(None, 'gx', 'gy', 'gz'), may hold values from -3 to 3
- density: float32 [8, 4, 8, 128], P('gx', 'gy', 'gz'), may hold values from 0.98 to 1.02
- mass: float32 [8, 4, 8, 128], P('gx', 'gy', 'gz'), may hold values from 0.008 to 0.024
- occupancy: int32 [8, 4, 8], P('gx', 'gy', 'gz'), may hold values from 32 to 128, as said below
- move_direction: int32 [8, 4, 8, 128], P('gx', 'gy', 'gz'), may hold values from 0 to 2, as said below
- move_slot: int32 [8, 4, 8, 128], P('gx', 'gy', 'gz'), may hold values from 0 to 127, as said below
Outputs:
- position_next: float32 [3, 8, 4, 8, 128], P(None, 'gx', 'gy', 'gz')
- velocity_next: float32 [3, 8, 4, 8, 128], P(None, 'gx', 'gy', 'gz')
- density_next: float32 [8, 4, 8, 128], P('gx', 'gy', 'gz')
- arrivals: float32 [7, 2, 4, 2, 4, 128], P(None, None, 'gx', 'gy', 'gz')
The draws below stay inside these ranges and needn't reach their ends.
Inputs may be any that keep to these rules, and one draw needn't show every extreme that they name: Slots 0 to occupancy - 1 of a cell are live; some cell has all 128 slots live. `move_direction`: 0 on every slot that is not live. `move_slot`: among the live particles of one device with the same nonzero move_direction the slots are distinct, so at most 128 leave a device in one direction; some device sends exactly 128 in one direction. 0 where move_direction is 0.
All inputs are finite; a program needn't handle non-finite values.
Results may differ from the reference program's by a relative error of at most 0.0003.
Values sent between devices are 32-bit elements; how exact they have to be, the bound alone decides.
No kernel may reach another device: no remote copies, remote signals or barrier semaphores. Data moves between devices by JAX's collectives and lax.ppermute only.
A program may use at most 64 MiB of HBM per device.

```python
import functools
import math
import jax
import jax.numpy as jnp
from jax import lax

SLOTS = 128
MOVES = 128
CX = 2
CY = 2
CZ = 2
NX = 8
NY = 4
NZ = 8
N_GX = 4
N_GY = 2
N_GZ = 4


def to_grid(values):
    shaped = values.reshape(N_GX, N_GY, N_GZ, CX, CY, CZ, SLOTS)
    shaped = shaped.transpose(0, 3, 1, 4, 2, 5, 6)
    return shaped.reshape(N_GX * CX, N_GY * CY, N_GZ * CZ, SLOTS)


def to_grid_cells(values):
    shaped = values.reshape(N_GX, N_GY, N_GZ, CX, CY, CZ)
    shaped = shaped.transpose(0, 3, 1, 4, 2, 5)
    return shaped.reshape(N_GX * CX, N_GY * CY, N_GZ * CZ)


def layout(key):
    devices_all = N_GX * N_GY * N_GZ
    cells = CX * CY * CZ
    places = cells * SLOTS
    keys = jax.random.split(key, 5)
    counts = jax.random.randint(keys[0], (devices_all * cells,), SLOTS // 4, SLOTS + 1)
    chosen_cell = jax.random.randint(keys[1], (), 0, devices_all * cells)
    counts = jnp.where(jnp.arange(devices_all * cells) == chosen_cell, SLOTS, counts).reshape(devices_all, cells)
    live = (jnp.arange(SLOTS)[None, None, :] < counts[:, :, None]).reshape(devices_all, places)
    leavers = jax.random.randint(keys[2], (devices_all * 2,), MOVES // 4, MOVES + 1)
    chosen_pair = jax.random.randint(keys[3], (), 0, devices_all * 2)
    leavers = jnp.where(jnp.arange(devices_all * 2) == chosen_pair, MOVES, leavers).reshape(devices_all, 2)
    scores = jax.random.randint(keys[4], (devices_all, places), 0, 4096) * places + jnp.arange(places)[None, :]
    scores = jnp.where(live, scores, scores + 4096 * places)
    order = jnp.argsort(scores, axis=1)
    ranking = jnp.argsort(order, axis=1).astype(jnp.int32)
    first = leavers[:, 0:1]
    second = leavers[:, 1:2]
    direction = jnp.where(ranking < first, 1, jnp.where(ranking < first + second, 2, 0)).astype(jnp.int32)
    target = jnp.where(direction == 1, ranking, jnp.where(direction == 2, ranking - first, 0)).astype(jnp.int32)
    return (to_grid_cells(counts).astype(jnp.int32), to_grid(direction), to_grid(target))


def draw_occupancy(key, part):
    return layout(jax.random.fold_in(key, 17))[0]


def draw_move_direction(key, part):
    return layout(jax.random.fold_in(key, 17))[1]


def draw_move_slot(key, part):
    return layout(jax.random.fold_in(key, 17))[2]


def level_of(key, dims, cuts, least, top_value):
    gain, own = 1.0, jax.random.fold_in(key, 6)
    for axis_at, blocks in cuts:
        heights = jnp.exp(jax.random.uniform(jax.random.fold_in(own, axis_at), (blocks,), jnp.float32, least / len(cuts), top_value / len(cuts)))
        gain = gain * jnp.repeat(heights, dims[axis_at] // blocks).reshape([-1 if axis == axis_at else 1 for axis in range(len(dims))])
    return gain


def bell_draw(rng, extent, deviation, reach, cuts=(), held_as=jnp.bfloat16):
    values = deviation * jax.random.normal(rng, extent, jnp.float32)
    if cuts:
        values = values * level_of(rng, extent, cuts, -0.22, 0.18)
    return jnp.clip(values, -reach, reach).astype(held_as)


def setup_inputs(seed: int = 0) -> dict:
    seeds = jax.random.split(jax.random.key(seed), 8)
    return {
        "offsets": jnp.clip(1.0 * jax.random.uniform(seeds[0], (3, NX, NY, NZ, SLOTS), jnp.float32) ** level_of(seeds[0], (3, NX, NY, NZ, SLOTS), ((1, 4), (2, 2), (3, 4)), -0.2, 0.2), 0.0, 1.0),
        "velocity": bell_draw(seeds[1], (3, NX, NY, NZ, SLOTS), 0.5, 3.0, ((1, 4), (2, 2), (3, 4)), jnp.float32),
        "density": jnp.clip(0.98 + 0.03999996 * jax.random.uniform(seeds[2], (NX, NY, NZ, SLOTS), jnp.float32) ** level_of(seeds[2], (NX, NY, NZ, SLOTS), ((0, 4), (1, 2), (2, 4)), -0.2, 0.2), 0.98, 1.02),
        "mass": jnp.clip(jnp.exp(math.log(0.024) - 1.09861225 * jax.random.uniform(seeds[3], (NX, NY, NZ, SLOTS), jnp.float32) ** level_of(seeds[3], (NX, NY, NZ, SLOTS), ((0, 4), (1, 2), (2, 4)), -0.2, 0.2)), 0.008, 0.024),
        "occupancy": draw_occupancy(jax.random.fold_in(seeds[7], 71), 0),
        "move_direction": draw_move_direction(jax.random.fold_in(seeds[7], 71), 0),
        "move_slot": draw_move_slot(jax.random.fold_in(seeds[7], 71), 0),
    }


SMOOTH = 0.5
KERNEL_NORM = 21.0 / (16.0 * math.pi * SMOOTH ** 3)
GRADIENT = 5.0 * KERNEL_NORM / SMOOTH ** 2
SOUND_SPEED = 10.0
STIFFNESS = SOUND_SPEED ** 2 / 7.0
VISCOSITY = 0.1
GRAVITY = 1.0
TIME_STEP = 0.1
HALF_STEP = 0.05

def pair_terms(own, near, shift):
    own_pos, own_vel, own_rho, own_mass = own
    near_pos, near_vel, near_rho, near_mass = near
    own_safe = jnp.where(own_mass > 0, own_rho, 1.0)
    near_safe = jnp.where(near_mass > 0, near_rho, 1.0)
    own_term = STIFFNESS * (own_safe ** 7 - 1.0) / (own_safe * own_safe)
    near_term = STIFFNESS * (near_safe ** 7 - 1.0) / (near_safe * near_safe)
    separation = [own_pos[part][:, :, None] - near_pos[part][:, None, :] - shift[part] for part in range(3)]
    relative = [own_vel[part][:, :, None] - near_vel[part][:, None, :] for part in range(3)]
    dist_sq = separation[0] * separation[0] + separation[1] * separation[1] + separation[2] * separation[2]
    along = relative[0] * separation[0] + relative[1] * separation[1] + relative[2] * separation[2]
    falloff = jnp.maximum(1.0 - 0.5 * jnp.sqrt(dist_sq) / SMOOTH, 0.0)
    weight = -GRADIENT * falloff * falloff * falloff * near_mass[:, None, :]
    closing = jnp.minimum(along, 0.0) / (dist_sq + 0.01 * SMOOTH * SMOOTH)
    viscous = -VISCOSITY * SOUND_SPEED * SMOOTH * closing / (0.5 * (own_safe[:, :, None] + near_safe[:, None, :]))
    push = weight * (own_term[:, :, None] + near_term[:, None, :] + viscous)
    accel = jnp.stack([-lax.optimization_barrier(jnp.sum(push * separation[part], axis=2)) for part in range(3)])
    density_rate = lax.optimization_barrier(jnp.sum(weight * along, axis=2))
    return (accel, density_rate)

def row_rates(block):
    cells_y = block.shape[2] - 2
    cells_z = block.shape[3] - 2
    slots = block.shape[4]
    centre = block[:, 1, 1:-1, 1:-1].reshape(8, -1, slots)
    own = (centre[0:3], centre[3:6], centre[6], centre[7])
    accel = jnp.zeros((3, cells_y * cells_z, slots), jnp.float32)
    density_rate = jnp.zeros((cells_y * cells_z, slots), jnp.float32)
    for shift_x in (-1, 0, 1):
        for shift_y in (-1, 0, 1):
            for shift_z in (-1, 0, 1):
                near = block[:, 1 + shift_x, 1 + shift_y:1 + shift_y + cells_y, 1 + shift_z:1 + shift_z + cells_z]
                near = near.reshape(8, -1, slots)
                part_accel, part_rate = pair_terms(own, (near[0:3], near[3:6], near[6], near[7]), (float(shift_x), float(shift_y), float(shift_z)))
                accel = accel + part_accel
                density_rate = density_rate + part_rate
    accel = accel - jnp.array([0.0, 0.0, GRAVITY], jnp.float32)[:, None, None]
    return (accel.reshape(3, cells_y, cells_z, slots), density_rate.reshape(cells_y, cells_z, slots))

def rates(padded):
    rows = padded.shape[1] - 2

    def one_row(row_index):
        return row_rates(lax.dynamic_slice_in_dim(padded, row_index, 3, 1))
    accel, density_rate = lax.map(one_row, jnp.arange(rows, dtype=jnp.int32))
    return (jnp.moveaxis(accel, 0, 1), density_rate)

def pack_moves(record, direction, target, alive, which, places_out):
    chosen = alive & (direction == which)
    where_to = jnp.where(chosen, target, places_out).astype(jnp.int32)
    summed = jax.ops.segment_sum(record.T, where_to, num_segments=places_out + 1)
    return summed[:places_out].T

def per_device(values):
    leading = values.shape[0]
    shaped = values.reshape(leading, N_GX, CX, N_GY, CY, N_GZ, CZ, SLOTS)
    shaped = shaped.transpose(1, 3, 5, 0, 2, 4, 6, 7)
    return shaped.reshape(N_GX * N_GY * N_GZ, leading, CX * CY * CZ * SLOTS)

def reference(offsets, velocity, density, mass, occupancy, move_direction, move_slot):
    live = jnp.arange(SLOTS, dtype=jnp.int32)[None, None, None, :] < occupancy[..., None]
    carried = jnp.where(live, mass, 0.0)
    fields = jnp.concatenate([offsets, velocity, density[None], carried[None]], 0)
    padding = ((0, 0), (1, 1), (1, 1), (1, 1), (0, 0))
    accel_first, rate_first = rates(jnp.pad(fields, padding))
    half_velocity = velocity + HALF_STEP * accel_first
    half = jnp.concatenate([offsets + HALF_STEP * velocity, half_velocity, (density + HALF_STEP * rate_first)[None], carried[None]], 0)
    accel_second, rate_second = rates(jnp.pad(half, padding))
    new_position = offsets + TIME_STEP * half_velocity
    new_velocity = velocity + TIME_STEP * accel_second
    new_density = density + TIME_STEP * rate_second
    stay = live & (move_direction == 0)
    position_next = jnp.where(stay[None], new_position, 0.0)
    velocity_next = jnp.where(stay[None], new_velocity, 0.0)
    density_next = jnp.where(stay, new_density, 0.0)
    grid_x = (jnp.arange(NX, dtype=jnp.int32) % CX).astype(jnp.float32)[:, None, None, None]
    grid_y = (jnp.arange(NY, dtype=jnp.int32) % CY).astype(jnp.float32)[None, :, None, None]
    grid_z = (jnp.arange(NZ, dtype=jnp.int32) % CZ).astype(jnp.float32)[None, None, :, None]
    shape = density.shape
    block_position = new_position + jnp.stack([jnp.broadcast_to(grid_x, shape), jnp.broadcast_to(grid_y, shape), jnp.broadcast_to(grid_z, shape)])
    record = jnp.concatenate([block_position, new_velocity, new_density[None]], 0)
    down_record = jnp.concatenate([record[0:1] - float(CX), record[1:]], 0)
    up_record = jnp.concatenate([record[0:1] + float(CX), record[1:]], 0)
    flat_dir = per_device(move_direction[None])[:, 0]
    flat_slot = per_device(move_slot[None])[:, 0]
    flat_live = per_device(live[None].astype(jnp.int32))[:, 0] > 0
    pack_down = functools.partial(pack_moves, which=1, places_out=MOVES)
    pack_up = functools.partial(pack_moves, which=2, places_out=MOVES)
    down = jax.vmap(pack_down)(per_device(down_record), flat_dir, flat_slot, flat_live)
    upper = jax.vmap(pack_up)(per_device(up_record), flat_dir, flat_slot, flat_live)
    down = down.reshape(N_GX, N_GY, N_GZ, 7, MOVES)
    upper = upper.reshape(N_GX, N_GY, N_GZ, 7, MOVES)
    zeros_row = jnp.zeros((1, N_GY, N_GZ, 7, MOVES), jnp.float32)
    from_lower = jnp.concatenate([zeros_row, down[:-1]], 0)
    from_upper = jnp.concatenate([upper[1:], zeros_row], 0)
    arrivals = jnp.stack([from_lower, from_upper], 0).transpose(4, 0, 1, 2, 3, 5)
    return (position_next, velocity_next, density_next, arrivals)
```

```python
import functools
import math

import jax
import jax.numpy as jnp
from jax import lax
from jax.experimental import pallas as pl
from jax.experimental.pallas import tpu as pltpu
from jax.sharding import PartitionSpec as P

MOVES = 128

SMOOTH = 0.5
KERNEL_NORM = 21.0 / (16.0 * math.pi * SMOOTH**3)
GRADIENT = 5.0 * KERNEL_NORM / SMOOTH**2
SOUND_SPEED = 10.0
STIFFNESS = SOUND_SPEED**2 / 7.0
VISCOSITY = 0.1
GRAVITY = 1.0
TIME_STEP = 0.1
HALF_STEP = 0.05

FIELDS = 8
TINY = 1e-24
VISC_SCALE = 2.0 * VISCOSITY * SOUND_SPEED * SMOOTH
SOFTENING = 0.01 * SMOOTH * SMOOTH
REACH = 2.0 * SMOOTH


def exchange(tiles, axis, dim):
    count, length = lax.axis_size(axis), tiles.shape[dim]
    last = lax.slice_in_dim(tiles, length - 1, length, axis=dim)
    first = lax.slice_in_dim(tiles, 0, 1, axis=dim)
    at = lax.axis_index(axis)
    if count == 1:
        before = after = jnp.zeros_like(first)
    elif count == 2:
        got = lax.ppermute(jnp.where(at == 0, last, first), axis, [(0, 1), (1, 0)])
        before = jnp.where(at == 0, 0.0, got)
        after = jnp.where(at == 0, got, 0.0)
    else:
        before = lax.ppermute(last, axis, [(i, (i + 1) % count) for i in range(count)])
        after = lax.ppermute(first, axis, [(i, (i - 1) % count) for i in range(count)])
        before = jnp.where(at == 0, 0.0, before)
        after = jnp.where(at == count - 1, 0.0, after)
    return jnp.concatenate([before, tiles, after], axis=dim)


def with_halo(tiles):
    for axis, dim in (("gy", 1), ("gz", 2), ("gx", 0)):
        tiles = exchange(tiles, axis, dim)
    return tiles


def pair_rates(halo_ref, counts, near, aux, own, total, cell, cells, write):
    cx, cy, cz = cell
    lane = lax.broadcasted_iota(jnp.int32, (FIELDS, 128), 1)
    row = lax.broadcasted_iota(jnp.int32, (FIELDS, 128), 0)
    at = jnp.int32(0)
    current = jnp.zeros((FIELDS, 128), jnp.float32)
    for sx in range(3):
        for sy in range(3):
            for sz in range(3):
                tile = halo_ref[cx + sx, cy + sy, cz + sz]
                shift = jnp.where(row == 0, sx - 1.0, jnp.where(row == 1, sy - 1.0, jnp.where(row == 2, sz - 1.0, 0.0)))
                here = counts[cx + sx, cy + sy, cz + sz]
                block, inside = at // 128, at % 128
                rolled = pltpu.roll(tile + shift, inside, axis=1)
                current = jnp.where(lane >= inside, rolled, current)
                near[block] = current
                near[block + 1] = rolled
                current = jnp.where(inside + here >= 128, rolled, current)
                at = at + here
    block, inside = at // 128, at % 128
    near[block] = jnp.where(lane < inside, current, 0.0)
    near[block + 1] = jnp.zeros_like(current)
    blocks = (at + 255) // 256

    def derive(index, carry):
        tile = near[index]
        rho, mass = tile[6:7], tile[7:8]
        safe = jnp.where(mass > 0, rho, 1.0)
        square = safe * safe
        sixth = square * square * square
        term = STIFFNESS * (sixth * safe - 1.0) / square
        aux[index] = jnp.concatenate([term, safe / VISC_SCALE, GRADIENT * mass] + [jnp.zeros_like(rho)] * 5, 0)
        return carry

    lax.fori_loop(0, 2 * blocks, derive, 0)
    tile = halo_ref[cx + 1, cy + 1, cz + 1]
    rho, mass = tile[6:7], tile[7:8]
    safe = jnp.where(mass > 0, rho, 1.0)
    square = safe * safe
    term = STIFFNESS * (square * square * square * safe - 1.0) / square
    columns = jnp.transpose(jnp.concatenate([tile[0:6], term, safe / VISC_SCALE], 0))
    for field in range(FIELDS):
        own[field] = jnp.broadcast_to(columns[:, field : field + 1], (128, 128))
    total[...] = jnp.zeros_like(total)
    here = counts[cx + 1, cy + 1, cz + 1]
    chunks = (here + 31) // 32

    def run(rows):
        def step(index, carry):
            js = []
            for side in range(2):
                tile_at = near.at[2 * index + side]
                extra = aux.at[2 * index + side]
                js.append(
                    [jnp.broadcast_to(tile_at[k : k + 1], (8, 128)) for k in range(6)]
                    + [jnp.broadcast_to(extra[k : k + 1], (8, 128)) for k in range(3)]
                )
            for part in range(rows // 8):
                at_rows = pl.ds(8 * part, 8)
                xi, yi, zi, ui, vi, wi, ai, qi = [own[field, at_rows] for field in range(8)]
                sums = [total[k, at_rows] for k in range(4)]
                for xj, yj, zj, uj, vj, wj, aj, qj, mj in js:
                    dx, dy, dz = xi - xj, yi - yj, zi - zj
                    du, dv, dw = ui - uj, vi - vj, wi - wj
                    dist_sq = dx * dx + dy * dy + dz * dz
                    along = du * dx + dv * dy + dw * dz
                    safe_sq = jnp.maximum(dist_sq, TINY)
                    dist = safe_sq * lax.rsqrt(safe_sq)
                    fall = jnp.maximum(1.0 - dist / REACH, 0.0)
                    weight = fall * fall * fall * mj
                    viscous = jnp.minimum(along, 0.0) / ((dist_sq + SOFTENING) * (qi + qj))
                    push = weight * (ai + aj - viscous)
                    sums[0] += push * dx
                    sums[1] += push * dy
                    sums[2] += push * dz
                    sums[3] += weight * along
                for k in range(4):
                    total[k, at_rows] = sums[k]
            return carry

        lax.fori_loop(0, blocks, step, 0)

    for rows in (32, 64, 96, 128):
        pl.when(chunks == rows // 32)(functools.partial(run, rows))
    ones = jnp.ones((8, 128), jnp.float32)
    result = []
    for k in range(4):
        result.append(
            lax.dot_general(
                ones, total[k], (((1,), (1,)), ((), ())), precision=lax.Precision.HIGHEST, preferred_element_type=jnp.float32
            )[0:1]
        )
    live = lane[0:1] < here
    accel = [jnp.where(live, r, 0.0) for r in result[:3]]
    accel[2] = accel[2] - GRAVITY
    rate = jnp.where(live, -result[3], 0.0)
    write(accel, rate)


def count_cells(halo_ref, counts):
    for x in range(halo_ref.shape[0]):
        for y in range(halo_ref.shape[1]):
            for z in range(halo_ref.shape[2]):
                counts[x, y, z] = jnp.sum((halo_ref[x, y, z, 7:8] > 0).astype(jnp.float32)).astype(jnp.int32)


def over_cells(halo_ref, scratch, cells, visit):
    counts, near, aux, own, total = scratch
    count_cells(halo_ref, counts)

    def one(index, carry):
        cx, cy, cz = index // (cells[1] * cells[2]), index // cells[2] % cells[1], index % cells[2]
        pair_rates(halo_ref, counts, near, aux, own, total, (cx, cy, cz), cells, functools.partial(visit, cx, cy, cz))
        return carry

    lax.fori_loop(0, cells[0] * cells[1] * cells[2], one, 0)


def half_kernel(cells, halo_ref, half_ref, *scratch):
    def visit(cx, cy, cz, accel, rate):
        tile = halo_ref[cx + 1, cy + 1, cz + 1]
        change = jnp.concatenate([tile[3:6]] + accel + [rate, jnp.zeros_like(rate)], 0)
        half_ref[cx, cy, cz] = tile + HALF_STEP * change

    over_cells(halo_ref, scratch, cells, visit)


def last_kernel(cells, halo_ref, state_ref, new_ref, *scratch):
    def visit(cx, cy, cz, accel, rate):
        tile = state_ref[cx, cy, cz]
        half = halo_ref[cx + 1, cy + 1, cz + 1]
        change = jnp.concatenate([half[3:6]] + accel + [rate, jnp.zeros_like(rate)], 0)
        new_ref[cx, cy, cz] = tile + TIME_STEP * change

    over_cells(halo_ref, scratch, cells, visit)


def scratch_for(halo_shape):
    return [
        pltpu.SMEM(halo_shape[:3], jnp.int32),
        pltpu.VMEM((30, FIELDS, 128), jnp.float32),
        pltpu.VMEM((30, FIELDS, 128), jnp.float32),
        pltpu.VMEM((FIELDS, 128, 128), jnp.float32),
        pltpu.VMEM((4, 128, 128), jnp.float32),
    ]


def call(kernel, halo, *others, cells):
    whole = pl.BlockSpec(memory_space=pltpu.VMEM)
    return pl.pallas_call(
        functools.partial(kernel, cells),
        out_shape=jax.ShapeDtypeStruct((*cells, FIELDS, 128), jnp.float32),
        in_specs=[whole] * (1 + len(others)),
        out_specs=whole,
        scratch_shapes=scratch_for(halo.shape),
    )(halo, *others)


def split3(values):
    high = values.astype(jnp.bfloat16)
    left = values - high.astype(jnp.float32)
    middle = left.astype(jnp.bfloat16)
    return high, middle, (left - middle.astype(jnp.float32)).astype(jnp.bfloat16)


def pack_kernel(cells, new_ref, direction_ref, slot_ref, occupancy_ref, out_ref):
    slots = lax.broadcasted_iota(jnp.int32, (2 * MOVES, 128), 0)
    lane = lax.broadcasted_iota(jnp.int32, (1, 128), 1)
    row = lax.broadcasted_iota(jnp.int32, (FIELDS, 128), 0)
    summed = jnp.zeros((FIELDS, 2 * MOVES), jnp.float32)
    for cx in range(cells[0]):
        for cy in range(cells[1]):
            for cz in range(cells[2]):
                live = lane < occupancy_ref[cx, cy, cz]
                way = jnp.where(live, direction_ref[cx, cy, cz : cz + 1], 0)
                slot = slot_ref[cx, cy, cz : cz + 1]
                target = jnp.where(way == 1, slot, jnp.where(way == 2, slot + MOVES, -1))
                chosen = (slots == target).astype(jnp.float32).astype(jnp.bfloat16)
                place = jnp.where(row == 0, float(cx), jnp.where(row == 1, float(cy), jnp.where(row == 2, float(cz), 0.0)))
                record = jnp.where(row == 7, 1.0, new_ref[cx, cy, cz] + place)
                for piece in split3(record):
                    summed += lax.dot_general(
                        piece, chosen, (((1,), (1,)), ((), ())), preferred_element_type=jnp.float32
                    )
    used = summed[7:8]
    side = lax.broadcasted_iota(jnp.int32, (1, 2 * MOVES), 1)
    moved = jnp.where(side < MOVES, -float(cells[0]), float(cells[0])) * used
    out_ref[...] = jnp.concatenate([summed[0:1] + moved, summed[1:]], 0)


def body(offsets, velocity, density, mass, occupancy, move_direction, move_slot):
    cells = density.shape[:3]
    slots = density.shape[3]
    live = jnp.arange(slots, dtype=jnp.int32)[None, None, None, :] < occupancy[..., None]
    carried = jnp.where(live, mass, 0.0)
    state = jnp.moveaxis(jnp.concatenate([offsets, velocity, density[None], carried[None]], 0), 0, 3)
    half = call(half_kernel, with_halo(state), cells=cells)
    new = call(last_kernel, with_halo(half), state, cells=cells)
    stay = live & (move_direction == 0)
    fields = jnp.where(stay[None], jnp.moveaxis(new, 3, 0), 0.0)
    whole = pl.BlockSpec(memory_space=pltpu.VMEM)
    packed = pl.pallas_call(
        functools.partial(pack_kernel, cells),
        out_shape=jax.ShapeDtypeStruct((FIELDS, 2 * MOVES), jnp.float32),
        in_specs=[whole, whole, whole, pl.BlockSpec(memory_space=pltpu.SMEM)],
        out_specs=whole,
    )(new, move_direction, move_slot, occupancy)
    count, at = lax.axis_size("gx"), lax.axis_index("gx")
    lists = jnp.zeros((FIELDS, 2, MOVES), jnp.float32)
    if count > 1:
        lower = lax.ppermute(packed[:, :MOVES], "gx", [(i, (i + 1) % count) for i in range(count)])
        upper = lax.ppermute(packed[:, MOVES:], "gx", [(i, (i - 1) % count) for i in range(count)])
        lists = jnp.stack([jnp.where(at == 0, 0.0, lower), jnp.where(at == count - 1, 0.0, upper)], 1)
    arrivals = lists[:7].reshape(7, 2, 1, 1, 1, MOVES)
    return (fields[0:3], fields[3:6], fields[6], arrivals)


def solution(mesh):
    placed = (
        P(None, "gx", "gy", "gz", None),
        P(None, "gx", "gy", "gz", None),
        P("gx", "gy", "gz", None),
        P("gx", "gy", "gz", None),
        P("gx", "gy", "gz"),
        P("gx", "gy", "gz", None),
        P("gx", "gy", "gz", None),
    )
    return jax.shard_map(
        body,
        mesh=mesh,
        in_specs=placed,
        out_specs=(
            P(None, "gx", "gy", "gz", None),
            P(None, "gx", "gy", "gz", None),
            P("gx", "gy", "gz", None),
            P(None, None, "gx", "gy", "gz", None),
        ),
        check_vma=False,
    )
```

```python
import functools
import math

import jax
import jax.numpy as jnp
from jax import lax
from jax.experimental import pallas as pl
from jax.experimental.pallas import tpu as pltpu
from jax.sharding import PartitionSpec as P

MOVES = 128

SMOOTH = 0.5
KERNEL_NORM = 21.0 / (16.0 * math.pi * SMOOTH**3)
GRADIENT = 5.0 * KERNEL_NORM / SMOOTH**2
SOUND_SPEED = 10.0
STIFFNESS = SOUND_SPEED**2 / 7.0
VISCOSITY = 0.1
GRAVITY = 1.0
TIME_STEP = 0.1
HALF_STEP = 0.05

FIELDS = 8
TINY = 1e-24
VISC_SCALE = 2.0 * VISCOSITY * SOUND_SPEED * SMOOTH
SOFTENING = 0.01 * SMOOTH * SMOOTH
REACH = 2.0 * SMOOTH


def exchange(tiles, axis, dim):
    count, length = lax.axis_size(axis), tiles.shape[dim]
    last = lax.slice_in_dim(tiles, length - 1, length, axis=dim)
    first = lax.slice_in_dim(tiles, 0, 1, axis=dim)
    at = lax.axis_index(axis)
    if count == 1:
        before = after = jnp.zeros_like(first)
    elif count == 2:
        got = lax.ppermute(jnp.where(at == 0, last, first), axis, [(0, 1), (1, 0)])
        before = jnp.where(at == 0, 0.0, got)
        after = jnp.where(at == 0, got, 0.0)
    else:
        before = lax.ppermute(last, axis, [(i, (i + 1) % count) for i in range(count)])
        after = lax.ppermute(first, axis, [(i, (i - 1) % count) for i in range(count)])
        before = jnp.where(at == 0, 0.0, before)
        after = jnp.where(at == count - 1, 0.0, after)
    return jnp.concatenate([before, tiles, after], axis=dim)


def with_halo(tiles):
    for axis, dim in (("gy", 1), ("gz", 2), ("gx", 0)):
        tiles = exchange(tiles, axis, dim)
    return tiles


def split3(values):
    high = values.astype(jnp.bfloat16).astype(jnp.float32)
    left = values - high
    middle = left.astype(jnp.bfloat16).astype(jnp.float32)
    return high, middle, left - middle


def squares(tile):
    product = tile * tile
    mixed = tile[0:3] * tile[3:6]
    return product[0:1] + product[1:2] + product[2:3], mixed[0:1] + mixed[1:2] + mixed[2:3]


def near_side(tile):
    high, middle, low = split3(tile)
    square, mixed = squares(tile)
    zero = jnp.zeros_like(square)
    extra = jnp.concatenate([square, mixed] + [zero] * 6, 0)
    row = lax.broadcasted_iota(jnp.int32, extra.shape, 0)
    extra_high, extra_middle, extra_low = split3(extra)
    extra_high = jnp.where((row >= 2) & (row < 5), 1.0, extra_high)
    pieces = [high, middle, low, high, middle, high, extra_high, extra_middle, extra_low, jnp.zeros_like(tile)]
    return jnp.concatenate(pieces, 0).astype(jnp.bfloat16)


def own_side(tile):
    square, mixed = squares(tile)
    zero, one = jnp.zeros_like(square), jnp.ones_like(square)
    sides = []
    for factors, value, marks in (
        (jnp.concatenate([-2.0 * tile[0:3]] + [zero] * 5, 0), square, [one, zero]),
        (-jnp.concatenate([tile[3:6], tile[0:3], zero, zero], 0), mixed, [zero, one]),
    ):
        high, middle, low = split3(factors)
        rest = jnp.concatenate(marks + [zero] * 6, 0)
        first = jnp.concatenate(marks + list(split3(value)) + [zero] * 3, 0)
        pieces = [high, high, high, middle, middle, low, first, rest, rest] + [jnp.zeros_like(factors)] * 7
        sides.append(jnp.transpose(jnp.concatenate(pieces, 0)))
    return jnp.concatenate(sides, 0).astype(jnp.bfloat16)


def pressure_rows(tile):
    rho, mass = tile[6:7], tile[7:8]
    safe = jnp.where(mass > 0, rho, 1.0)
    square = safe * safe
    return safe * (1.0 / VISC_SCALE), STIFFNESS * (square * square * square * safe - 1.0) / square


def count_cells(halo_ref, counts):
    for x in range(halo_ref.shape[0]):
        for y in range(halo_ref.shape[1]):
            for z in range(halo_ref.shape[2]):
                counts[x, y, z] = jnp.sum((halo_ref[x, y, z, 7:8] > 0).astype(jnp.float32)).astype(jnp.int32)


def compact(halo_ref, counts, near, blocks, cells):
    lane = lax.broadcasted_iota(jnp.int32, (FIELDS, 128), 1)
    row = lax.broadcasted_iota(jnp.int32, (FIELDS, 128), 0)
    places = [(x, y, z) for x in range(cells[0]) for y in range(cells[1]) for z in range(cells[2])]
    at = [jnp.int32(0)] * len(places)
    current = [jnp.zeros((FIELDS, 128), jnp.float32)] * len(places)
    for sx in range(3):
        for sy in range(3):
            for sz in range(3):
                shift = jnp.where(row == 0, sx - 1.5, jnp.where(row == 1, sy - 1.5, jnp.where(row == 2, sz - 1.5, 0.0)))
                for c, (cx, cy, cz) in enumerate(places):
                    block, inside = lax.shift_right_logical(at[c], 7), at[c] & 127
                    rolled = pltpu.roll(halo_ref[cx + sx, cy + sy, cz + sz] + shift, inside, axis=1)
                    merged = jnp.where(lane >= inside, rolled, current[c])
                    near[c, block] = merged
                    near[c, block + 1] = rolled
                    at[c] = at[c] + counts[cx + sx, cy + sy, cz + sz]
                    current[c] = jnp.where(lax.shift_right_logical(at[c], 7) != block, rolled, merged)
    for c in range(len(places)):
        block, inside = lax.shift_right_logical(at[c], 7), at[c] & 127
        near[c, block] = jnp.where(lane < inside, current[c], 0.0)
        near[c, block + 1] = jnp.zeros_like(current[c])
        blocks[c] = lax.shift_right_logical(at[c] + 255, 8)


def pair_sums(halo_ref, counts, near, blocks, own, terms, slots, total, cell, index):
    cx, cy, cz = cell
    row = lax.broadcasted_iota(jnp.int32, (FIELDS, 128), 0)
    tile = halo_ref[cx + 1, cy + 1, cz + 1] - jnp.where(row < 3, 0.5, 0.0)
    own[...] = own_side(tile)
    columns = jnp.transpose(jnp.concatenate(list(pressure_rows(tile)) + [jnp.zeros((6, 128), jnp.float32)], 0))
    for k in range(2):
        terms[k] = jnp.broadcast_to(columns[:, k : k + 1], (128, 128))
    total[index] = jnp.zeros(total.shape[1:], jnp.float32)
    here = counts[cx + 1, cy + 1, cz + 1]
    chunks = lax.shift_right_logical(here + 31, 5)
    count = blocks[index]

    def run(rows):
        def products(block, slot):
            right = jnp.concatenate([near_side(near[index, 2 * block]), near_side(near[index, 2 * block + 1])], 1)
            depth = right.shape[0]
            for k in range(2):
                slot[k, 0:rows] = jnp.dot(own[pl.ds(128 * k, rows), 0:depth], right, preferred_element_type=jnp.float32)

        def add(block, slot):
            js = []
            for side in range(2):
                listed = near[index, 2 * block + side]
                values = [listed[0:1], listed[1:2], listed[2:3], *pressure_rows(listed), GRADIENT * listed[7:8]]
                js.append([jnp.broadcast_to(value, (8, 128)) for value in values])
            for part in range(rows // 8):
                at = pl.ds(8 * part, 8)
                qi, ai = terms[0, at], terms[1, at]
                sums = [total[index, k, at] for k in range(5)]
                for side, (xj, yj, zj, qj, aj, mj) in enumerate(js):
                    lanes = pl.ds(128 * side, 128)
                    dist_sq, along = jnp.maximum(slot[0, at, lanes], TINY), slot[1, at, lanes]
                    dist = dist_sq * lax.rsqrt(dist_sq)
                    fall = jnp.maximum(1.0 - (dist if REACH == 1.0 else dist * (1.0 / REACH)), 0.0)
                    weight = fall * fall * fall * mj
                    viscous = jnp.minimum(along, 0.0) / ((dist_sq + SOFTENING) * (qi + qj))
                    push = weight * (ai + aj - viscous)
                    sums[0] += push
                    sums[1] += push * xj
                    sums[2] += push * yj
                    sums[3] += push * zj
                    sums[4] += weight * along
                for k in range(5):
                    total[index, k, at] = sums[k]

        products(0, slots[0])

        def step(pair, carry):
            products(2 * pair + 1, slots[1])
            add(2 * pair, slots[0])
            products(2 * pair + 2, slots[0])
            add(2 * pair + 1, slots[1])
            return carry

        lax.fori_loop(0, lax.shift_right_logical(count, 1), step, 0)

        @pl.when((count & 1) == 1)
        def _():
            add(count - 1, slots[0])

    for rows in (32, 64, 96, 128):
        pl.when(chunks == rows // 32)(functools.partial(run, rows))


def over_cells(halo_ref, scratch, cells, visit):
    counts, blocks, near, own, terms, slot_a, slot_b, total = scratch
    count_cells(halo_ref, counts)
    compact(halo_ref, counts, near, blocks, cells)

    def one(index, carry):
        cz = index % cells[2]
        cy = lax.div(index, cells[2]) % cells[1]
        cx = lax.div(index, cells[1] * cells[2])
        pair_sums(halo_ref, counts, near, blocks, own, terms, (slot_a, slot_b), total, (cx, cy, cz), index)
        return carry

    lax.fori_loop(0, cells[0] * cells[1] * cells[2], one, 0)
    ones = jnp.ones((16, 128), jnp.bfloat16)
    lane = lax.broadcasted_iota(jnp.int32, (1, 128), 1)
    for index in range(cells[0] * cells[1] * cells[2]):
        cx, cy, cz = index // (cells[1] * cells[2]), index // cells[2] % cells[1], index % cells[2]
        flat = total[index].reshape(5 * 128, 128)
        high = flat.astype(jnp.bfloat16)
        left = flat - high.astype(jnp.float32)
        middle = left.astype(jnp.bfloat16)
        summed = sum(
            lax.dot_general(ones, piece, (((1,), (1,)), ((), ())), preferred_element_type=jnp.float32)[0:1]
            for piece in (high, middle)
        )
        sums = [summed[:, 128 * k : 128 * (k + 1)] for k in range(5)]
        tile = halo_ref[cx + 1, cy + 1, cz + 1]
        live = lane < counts[cx + 1, cy + 1, cz + 1]
        accel = [jnp.where(live, (tile[k : k + 1] - 0.5) * sums[0] - sums[k + 1], 0.0) for k in range(3)]
        accel[2] = accel[2] - GRAVITY
        visit(cx, cy, cz, accel, jnp.where(live, -sums[4], 0.0))


def half_kernel(cells, halo_ref, half_ref, *scratch):
    def visit(cx, cy, cz, accel, rate):
        tile = halo_ref[cx + 1, cy + 1, cz + 1]
        change = jnp.concatenate([tile[3:6]] + accel + [rate, jnp.zeros_like(rate)], 0)
        half_ref[cx, cy, cz] = tile + HALF_STEP * change

    over_cells(halo_ref, scratch, cells, visit)


def last_kernel(cells, halo_ref, state_ref, new_ref, *scratch):
    def visit(cx, cy, cz, accel, rate):
        tile = state_ref[cx, cy, cz]
        half = halo_ref[cx + 1, cy + 1, cz + 1]
        change = jnp.concatenate([half[3:6]] + accel + [rate, jnp.zeros_like(rate)], 0)
        new_ref[cx, cy, cz] = tile + TIME_STEP * change

    over_cells(halo_ref, scratch, cells, visit)


def scratch_for(halo_shape, cells):
    own = cells[0] * cells[1] * cells[2]
    return [
        pltpu.SMEM(halo_shape[:3], jnp.int32),
        pltpu.SMEM((own,), jnp.int32),
        pltpu.VMEM((own, 32, FIELDS, 128), jnp.float32),
        pltpu.VMEM((256, 128), jnp.bfloat16),
        pltpu.VMEM((2, 128, 128), jnp.float32),
        pltpu.VMEM((2, 128, 256), jnp.float32),
        pltpu.VMEM((2, 128, 256), jnp.float32),
        pltpu.VMEM((own, 5, 128, 128), jnp.float32),
    ]


def call(kernel, halo, *others, cells):
    whole = pl.BlockSpec(memory_space=pltpu.VMEM)
    return pl.pallas_call(
        functools.partial(kernel, cells),
        out_shape=jax.ShapeDtypeStruct((*cells, FIELDS, 128), jnp.float32),
        in_specs=[whole] * (1 + len(others)),
        out_specs=whole,
        scratch_shapes=scratch_for(halo.shape, cells),
    )(halo, *others)


def pack_kernel(cells, new_ref, direction_ref, slot_ref, occupancy_ref, out_ref):
    slots = lax.broadcasted_iota(jnp.int32, (2 * MOVES, 128), 0)
    lane = lax.broadcasted_iota(jnp.int32, (1, 128), 1)
    row = lax.broadcasted_iota(jnp.int32, (FIELDS, 128), 0)
    summed = jnp.zeros((FIELDS, 2 * MOVES), jnp.float32)
    for cx in range(cells[0]):
        for cy in range(cells[1]):
            for cz in range(cells[2]):
                live = lane < occupancy_ref[cx, cy, cz]
                way = jnp.where(live, direction_ref[cx, cy, cz : cz + 1], 0)
                slot = slot_ref[cx, cy, cz : cz + 1]
                target = jnp.where(way == 1, slot, jnp.where(way == 2, slot + MOVES, -1))
                chosen = (slots == target).astype(jnp.float32).astype(jnp.bfloat16)
                place = jnp.where(row == 0, float(cx), jnp.where(row == 1, float(cy), jnp.where(row == 2, float(cz), 0.0)))
                record = jnp.where(row == 7, 1.0, new_ref[cx, cy, cz] + place)
                for piece in split3(record):
                    summed += lax.dot_general(
                        piece.astype(jnp.bfloat16), chosen, (((1,), (1,)), ((), ())), preferred_element_type=jnp.float32
                    )
    used = summed[7:8]
    side = lax.broadcasted_iota(jnp.int32, (1, 2 * MOVES), 1)
    moved = jnp.where(side < MOVES, -float(cells[0]), float(cells[0])) * used
    out_ref[...] = jnp.concatenate([summed[0:1] + moved, summed[1:]], 0)


def body(offsets, velocity, density, mass, occupancy, move_direction, move_slot):
    cells = density.shape[:3]
    slots = density.shape[3]
    live = jnp.arange(slots, dtype=jnp.int32)[None, None, None, :] < occupancy[..., None]
    carried = jnp.where(live, mass, 0.0)
    state = jnp.moveaxis(jnp.concatenate([offsets, velocity, density[None], carried[None]], 0), 0, 3)
    half = call(half_kernel, with_halo(state), cells=cells)
    new = call(last_kernel, with_halo(half), state, cells=cells)
    stay = live & (move_direction == 0)
    fields = jnp.where(stay[None], jnp.moveaxis(new, 3, 0), 0.0)
    whole = pl.BlockSpec(memory_space=pltpu.VMEM)
    packed = pl.pallas_call(
        functools.partial(pack_kernel, cells),
        out_shape=jax.ShapeDtypeStruct((FIELDS, 2 * MOVES), jnp.float32),
        in_specs=[whole, whole, whole, pl.BlockSpec(memory_space=pltpu.SMEM)],
        out_specs=whole,
    )(new, move_direction, move_slot, occupancy)
    count, at = lax.axis_size("gx"), lax.axis_index("gx")
    lists = jnp.zeros((FIELDS, 2, MOVES), jnp.float32)
    if count > 1:
        lower = lax.ppermute(packed[:, :MOVES], "gx", [(i, (i + 1) % count) for i in range(count)])
        upper = lax.ppermute(packed[:, MOVES:], "gx", [(i, (i - 1) % count) for i in range(count)])
        lists = jnp.stack([jnp.where(at == 0, 0.0, lower), jnp.where(at == count - 1, 0.0, upper)], 1)
    arrivals = lists[:7].reshape(7, 2, 1, 1, 1, MOVES)
    return (fields[0:3], fields[3:6], fields[6], arrivals)


def solution(mesh):
    placed = (
        P(None, "gx", "gy", "gz", None),
        P(None, "gx", "gy", "gz", None),
        P("gx", "gy", "gz", None),
        P("gx", "gy", "gz", None),
        P("gx", "gy", "gz"),
        P("gx", "gy", "gz", None),
        P("gx", "gy", "gz", None),
    )
    return jax.shard_map(
        body,
        mesh=mesh,
        in_specs=placed,
        out_specs=(
            P(None, "gx", "gy", "gz", None),
            P(None, "gx", "gy", "gz", None),
            P("gx", "gy", "gz", None),
            P(None, None, "gx", "gy", "gz", None),
        ),
        check_vma=False,
    )
```

```python
import functools
import math

import jax
import jax.numpy as jnp
from jax import lax
from jax.experimental import pallas as pl
from jax.experimental.pallas import tpu as pltpu
from jax.sharding import PartitionSpec as P

MOVES = 128

SMOOTH = 0.5
KERNEL_NORM = 21.0 / (16.0 * math.pi * SMOOTH**3)
GRADIENT = 5.0 * KERNEL_NORM / SMOOTH**2
SOUND_SPEED = 10.0
STIFFNESS = SOUND_SPEED**2 / 7.0
VISCOSITY = 0.1
GRAVITY = 1.0
TIME_STEP = 0.1
HALF_STEP = 0.05

FIELDS = 8
TINY = 1e-24
VISC_SCALE = 2.0 * VISCOSITY * SOUND_SPEED * SMOOTH
SOFTENING = 0.01 * SMOOTH * SMOOTH
REACH = 2.0 * SMOOTH


def exchange(tiles, axis, dim):
    count, length = lax.axis_size(axis), tiles.shape[dim]
    last = lax.slice_in_dim(tiles, length - 1, length, axis=dim)
    first = lax.slice_in_dim(tiles, 0, 1, axis=dim)
    at = lax.axis_index(axis)
    if count == 1:
        before = after = jnp.zeros_like(first)
    elif count == 2:
        got = lax.ppermute(jnp.where(at == 0, last, first), axis, [(0, 1), (1, 0)])
        before = jnp.where(at == 0, 0.0, got)
        after = jnp.where(at == 0, got, 0.0)
    else:
        before = lax.ppermute(last, axis, [(i, (i + 1) % count) for i in range(count)])
        after = lax.ppermute(first, axis, [(i, (i - 1) % count) for i in range(count)])
        before = jnp.where(at == 0, 0.0, before)
        after = jnp.where(at == count - 1, 0.0, after)
    return jnp.concatenate([before, tiles, after], axis=dim)


def with_halo(tiles):
    for axis, dim in (("gy", 1), ("gz", 2), ("gx", 0)):
        tiles = exchange(tiles, axis, dim)
    return tiles


def split3(values):
    high = values.astype(jnp.bfloat16).astype(jnp.float32)
    left = values - high
    middle = left.astype(jnp.bfloat16).astype(jnp.float32)
    return high, middle, left - middle


def squares(tile):
    product = tile * tile
    mixed = tile[0:3] * tile[3:6]
    return product[0:1] + product[1:2] + product[2:3], mixed[0:1] + mixed[1:2] + mixed[2:3]


def near_side(tile):
    high, middle, low = split3(tile)
    square, mixed = squares(tile)
    zero = jnp.zeros_like(square)
    extra = jnp.concatenate([square, mixed] + [zero] * 6, 0)
    row = lax.broadcasted_iota(jnp.int32, extra.shape, 0)
    extra_high, extra_middle, extra_low = split3(extra)
    extra_high = jnp.where((row >= 2) & (row < 5), 1.0, extra_high)
    pieces = [high, middle, low, high, middle, high, extra_high, extra_middle, extra_low, jnp.zeros_like(tile)]
    return jnp.concatenate(pieces, 0).astype(jnp.bfloat16)


def own_side(tile):
    square, mixed = squares(tile)
    zero, one = jnp.zeros_like(square), jnp.ones_like(square)
    sides = []
    for factors, value, marks in (
        (jnp.concatenate([-2.0 * tile[0:3]] + [zero] * 5, 0), square, [one, zero]),
        (-jnp.concatenate([tile[3:6], tile[0:3], zero, zero], 0), mixed, [zero, one]),
    ):
        high, middle, low = split3(factors)
        rest = jnp.concatenate(marks + [zero] * 6, 0)
        first = jnp.concatenate(marks + list(split3(value)) + [zero] * 3, 0)
        pieces = [high, high, high, middle, middle, low, first, rest, rest] + [jnp.zeros_like(factors)] * 7
        sides.append(jnp.transpose(jnp.concatenate(pieces, 0)))
    return jnp.concatenate(sides, 0).astype(jnp.bfloat16)


def pressure_rows(tile):
    rho, mass = tile[6:7], tile[7:8]
    safe = jnp.where(mass > 0, rho, 1.0)
    square = safe * safe
    return safe * (1.0 / VISC_SCALE), STIFFNESS * (square * square * square * safe - 1.0) / square


def count_cells(halo_ref, counts):
    for x in range(halo_ref.shape[0]):
        for y in range(halo_ref.shape[1]):
            for z in range(halo_ref.shape[2]):
                counts[x, y, z] = jnp.sum((halo_ref[x, y, z, 7:8] > 0).astype(jnp.float32)).astype(jnp.int32)


def compact(halo_ref, counts, near, blocks, cells):
    lane = lax.broadcasted_iota(jnp.int32, (FIELDS, 128), 1)
    row = lax.broadcasted_iota(jnp.int32, (FIELDS, 128), 0)
    places = all_cells(cells)
    at = [jnp.int32(0)] * len(places)
    current = [jnp.zeros((FIELDS, 128), jnp.float32)] * len(places)
    for sx in range(3):
        for sy in range(3):
            for sz in range(3):
                shift = jnp.where(row == 0, sx - 1.5, jnp.where(row == 1, sy - 1.5, jnp.where(row == 2, sz - 1.5, 0.0)))
                for c, (cx, cy, cz) in enumerate(places):
                    block, inside = lax.shift_right_logical(at[c], 7), at[c] & 127
                    rolled = pltpu.roll(halo_ref[cx + sx, cy + sy, cz + sz] + shift, inside, axis=1)
                    merged = jnp.where(lane >= inside, rolled, current[c])
                    near[c, block] = merged
                    near[c, block + 1] = rolled
                    at[c] = at[c] + counts[cx + sx, cy + sy, cz + sz]
                    current[c] = jnp.where(lax.shift_right_logical(at[c], 7) != block, rolled, merged)
    for c in range(len(places)):
        block, inside = lax.shift_right_logical(at[c], 7), at[c] & 127
        near[c, block] = jnp.where(lane < inside, current[c], 0.0)
        near[c, block + 1] = jnp.zeros_like(current[c])
        blocks[c] = lax.shift_right_logical(at[c] + 255, 8)


def pair_sums(halo_ref, counts, near, blocks, own, terms, slots, total, cell, index):
    cx, cy, cz = cell
    row = lax.broadcasted_iota(jnp.int32, (FIELDS, 128), 0)
    tile = halo_ref[cx + 1, cy + 1, cz + 1] - jnp.where(row < 3, 0.5, 0.0)
    own[...] = own_side(tile)
    columns = jnp.transpose(jnp.concatenate(list(pressure_rows(tile)) + [jnp.zeros((6, 128), jnp.float32)], 0))
    for k in range(2):
        terms[k] = jnp.broadcast_to(columns[:, k : k + 1], (128, 128))
    total[index] = jnp.zeros(total.shape[1:], jnp.float32)
    here = counts[cx + 1, cy + 1, cz + 1]
    chunks = lax.shift_right_logical(here + 31, 5)
    count = blocks[index]

    def run(rows):
        def products(block, slot):
            right = jnp.concatenate([near_side(near[index, 2 * block]), near_side(near[index, 2 * block + 1])], 1)
            depth = right.shape[0]
            for k in range(2):
                slot[k, 0:rows] = jnp.dot(own[pl.ds(128 * k, rows), 0:depth], right, preferred_element_type=jnp.float32)

        def add(block, slot):
            js = []
            for side in range(2):
                listed = near[index, 2 * block + side]
                values = [listed[0:1], listed[1:2], listed[2:3], *pressure_rows(listed), GRADIENT * listed[7:8]]
                js.append([jnp.broadcast_to(value, (8, 128)) for value in values])
            for part in range(rows // 8):
                at = pl.ds(8 * part, 8)
                qi, ai = terms[0, at], terms[1, at]
                sums = [total[index, k, at] for k in range(5)]
                for side, (xj, yj, zj, qj, aj, mj) in enumerate(js):
                    lanes = pl.ds(128 * side, 128)
                    dist_sq, along = jnp.maximum(slot[0, at, lanes], TINY), slot[1, at, lanes]
                    dist = dist_sq * lax.rsqrt(dist_sq)
                    fall = jnp.maximum(1.0 - (dist if REACH == 1.0 else dist * (1.0 / REACH)), 0.0)
                    weight = fall * fall * fall * mj
                    viscous = jnp.minimum(along, 0.0) / ((dist_sq + SOFTENING) * (qi + qj))
                    push = weight * (ai + aj - viscous)
                    sums[0] += push
                    sums[1] += push * xj
                    sums[2] += push * yj
                    sums[3] += push * zj
                    sums[4] += weight * along
                for k in range(5):
                    total[index, k, at] = sums[k]

        products(0, slots[0])

        def step(pair, carry):
            products(2 * pair + 1, slots[1])
            add(2 * pair, slots[0])
            products(2 * pair + 2, slots[0])
            add(2 * pair + 1, slots[1])
            return carry

        lax.fori_loop(0, lax.shift_right_logical(count, 1), step, 0)

        @pl.when((count & 1) == 1)
        def _():
            add(count - 1, slots[0])

    for rows in (32, 64, 96, 128):
        pl.when(chunks == rows // 32)(functools.partial(run, rows))


def over_cells(halo_ref, scratch, cells, visit):
    counts, blocks, near, own, terms, slot_a, slot_b, total = scratch
    count_cells(halo_ref, counts)
    compact(halo_ref, counts, near, blocks, cells)

    def one(index, carry):
        cz = index % cells[2]
        cy = lax.div(index, cells[2]) % cells[1]
        cx = lax.div(index, cells[1] * cells[2])
        pair_sums(halo_ref, counts, near, blocks, own, terms, (slot_a, slot_b), total, (cx, cy, cz), index)
        return carry

    lax.fori_loop(0, cells[0] * cells[1] * cells[2], one, 0)
    ones = jnp.ones((16, 128), jnp.bfloat16)
    lane = lax.broadcasted_iota(jnp.int32, (1, 128), 1)
    for index in range(cells[0] * cells[1] * cells[2]):
        cx, cy, cz = index // (cells[1] * cells[2]), index // cells[2] % cells[1], index % cells[2]
        flat = total[index].reshape(5 * 128, 128)
        high = flat.astype(jnp.bfloat16)
        left = flat - high.astype(jnp.float32)
        middle = left.astype(jnp.bfloat16)
        summed = sum(
            lax.dot_general(ones, piece, (((1,), (1,)), ((), ())), preferred_element_type=jnp.float32)[0:1]
            for piece in (high, middle)
        )
        sums = [summed[:, 128 * k : 128 * (k + 1)] for k in range(5)]
        tile = halo_ref[cx + 1, cy + 1, cz + 1]
        live = lane < counts[cx + 1, cy + 1, cz + 1]
        accel = [jnp.where(live, (tile[k : k + 1] - 0.5) * sums[0] - sums[k + 1], 0.0) for k in range(3)]
        accel[2] = accel[2] - GRAVITY
        visit(cx, cy, cz, accel, jnp.where(live, -sums[4], 0.0))


def scratch_for(halo_shape, cells):
    own = cells[0] * cells[1] * cells[2]
    return [
        pltpu.SMEM(halo_shape[:3], jnp.int32),
        pltpu.SMEM((own,), jnp.int32),
        pltpu.VMEM((own, 32, FIELDS, 128), jnp.float32),
        pltpu.VMEM((256, 128), jnp.bfloat16),
        pltpu.VMEM((2, 128, 128), jnp.float32),
        pltpu.VMEM((2, 128, 256), jnp.float32),
        pltpu.VMEM((2, 128, 256), jnp.float32),
        pltpu.VMEM((own, 5, 128, 128), jnp.float32),
    ]


def call(kernel, cells, outs, args, scratch=(), scalars=(), grant=16):
    whole = pl.BlockSpec(memory_space=pltpu.VMEM)
    table = pl.BlockSpec(memory_space=pltpu.SMEM)
    return pl.pallas_call(
        functools.partial(kernel, cells),
        out_shape=[out if hasattr(out, "dtype") else jax.ShapeDtypeStruct(out, jnp.float32) for out in outs],
        in_specs=[whole] * len(args) + [table] * len(scalars),
        out_specs=[whole] * len(outs),
        scratch_shapes=list(scratch),
        compiler_params=pltpu.CompilerParams(vmem_limit_bytes=grant * 1024 * 1024),
    )(*args, *scalars)


def all_cells(cells):
    return [(x, y, z) for x in range(cells[0]) for y in range(cells[1]) for z in range(cells[2])]


def state_kernel(
    cells, offsets_ref, velocity_ref, density_ref, mass_ref, direction_ref, slot_ref, occupancy_ref, state_ref, target_ref
):
    lane = lax.broadcasted_iota(jnp.int32, (1, 128), 1)
    for cx, cy, cz in all_cells(cells):
        here = pl.ds(cz, 1)
        for k in range(3):
            state_ref[cx, cy, cz, k : k + 1] = offsets_ref[k, cx, cy, here]
            state_ref[cx, cy, cz, k + 3 : k + 4] = velocity_ref[k, cx, cy, here]
        state_ref[cx, cy, cz, 6:7] = density_ref[cx, cy, here]
        live = lane < occupancy_ref[cx, cy, cz]
        state_ref[cx, cy, cz, 7:8] = jnp.where(live, mass_ref[cx, cy, here], 0.0)
        way, slot = direction_ref[cx, cy, here], slot_ref[cx, cy, here]
        target = jnp.where(way == 1, slot, jnp.where(way == 2, slot + MOVES, -1))
        target_ref[cx, cy, here] = jnp.where(live, target, -2)


def half_kernel(cells, halo_ref, half_ref, *scratch):
    def visit(cx, cy, cz, accel, rate):
        tile = halo_ref[cx + 1, cy + 1, cz + 1]
        change = jnp.concatenate([tile[3:6]] + accel + [rate, jnp.zeros_like(rate)], 0)
        half_ref[cx, cy, cz] = tile + HALF_STEP * change

    over_cells(halo_ref, scratch, cells, visit)


def last_kernel(
    cells, halo_ref, state_ref, target_ref, lower_ref, upper_ref, position_ref, velocity_ref, density_ref, *scratch
):
    slots = lax.broadcasted_iota(jnp.int32, (2 * MOVES, 128), 0)
    row = lax.broadcasted_iota(jnp.int32, (FIELDS, 128), 0)
    lists = [jnp.zeros((FIELDS, 2 * MOVES), jnp.float32)]

    def visit(cx, cy, cz, accel, rate):
        tile = state_ref[cx, cy, cz]
        half = halo_ref[cx + 1, cy + 1, cz + 1]
        change = jnp.concatenate([half[3:6]] + accel + [rate, jnp.zeros_like(rate)], 0)
        new = tile + TIME_STEP * change
        here = pl.ds(cz, 1)
        target = target_ref[cx, cy, here]
        kept = jnp.where(target == -1, new, 0.0)
        for k in range(3):
            position_ref[k, cx, cy, here] = kept[k : k + 1]
            velocity_ref[k, cx, cy, here] = kept[k + 3 : k + 4]
        density_ref[cx, cy, here] = kept[6:7]
        chosen = (slots == target).astype(jnp.float32).astype(jnp.bfloat16)
        place = jnp.where(row == 0, float(cx), jnp.where(row == 1, float(cy), jnp.where(row == 2, float(cz), 0.0)))
        record = jnp.where(row == 7, 1.0, new + place)
        for piece in split3(record):
            lists[0] += lax.dot_general(
                piece.astype(jnp.bfloat16), chosen, (((1,), (1,)), ((), ())), preferred_element_type=jnp.float32
            )

    over_cells(halo_ref, scratch, cells, visit)
    for side, (out_ref, moved) in enumerate(((lower_ref, -float(cells[0])), (upper_ref, float(cells[0])))):
        half = lists[0][:, MOVES * side : MOVES * (side + 1)]
        out_ref[...] = half + jnp.where(row == 0, moved, 0.0) * half[7:8]


def body(offsets, velocity, density, mass, occupancy, move_direction, move_slot):
    cells = density.shape[:3]
    tiles = (*cells, FIELDS, 128)
    fields = (offsets, velocity, density, mass, move_direction, move_slot)
    places = jax.ShapeDtypeStruct(density.shape, jnp.int32)
    state, target = call(state_kernel, cells, [tiles, places], fields, scalars=(occupancy,), grant=60)
    halo = with_halo(state)
    scratch = scratch_for(halo.shape, cells)
    (half,) = call(half_kernel, cells, [tiles], (halo,), scratch)
    outs = [(FIELDS, MOVES), (FIELDS, MOVES), offsets.shape, velocity.shape, density.shape]
    lower, upper, position_next, velocity_next, density_next = call(
        last_kernel, cells, outs, (with_halo(half), state, target), scratch
    )
    count, at = lax.axis_size("gx"), lax.axis_index("gx")
    if count > 1:
        lower = lax.ppermute(lower, "gx", [(i, (i + 1) % count) for i in range(count)])
        upper = lax.ppermute(upper, "gx", [(i, (i - 1) % count) for i in range(count)])
    lists = jnp.stack([jnp.where(at == 0, 0.0, lower), jnp.where(at == count - 1, 0.0, upper)], 1)
    arrivals = lists[:7].reshape(7, 2, 1, 1, 1, MOVES)
    return (position_next, velocity_next, density_next, arrivals)


def solution(mesh):
    placed = (
        P(None, "gx", "gy", "gz", None),
        P(None, "gx", "gy", "gz", None),
        P("gx", "gy", "gz", None),
        P("gx", "gy", "gz", None),
        P("gx", "gy", "gz"),
        P("gx", "gy", "gz", None),
        P("gx", "gy", "gz", None),
    )
    return jax.shard_map(
        body,
        mesh=mesh,
        in_specs=placed,
        out_specs=(
            P(None, "gx", "gy", "gz", None),
            P(None, "gx", "gy", "gz", None),
            P("gx", "gy", "gz", None),
            P(None, None, "gx", "gy", "gz", None),
        ),
        check_vma=False,
    )
```

```python
import functools
import math

import jax
import jax.numpy as jnp
from jax import lax
from jax.experimental import pallas as pl
from jax.experimental.pallas import tpu as pltpu
from jax.sharding import PartitionSpec as P

MOVES = 128

SMOOTH = 0.5
KERNEL_NORM = 21.0 / (16.0 * math.pi * SMOOTH**3)
GRADIENT = 5.0 * KERNEL_NORM / SMOOTH**2
SOUND_SPEED = 10.0
STIFFNESS = SOUND_SPEED**2 / 7.0
VISCOSITY = 0.1
GRAVITY = 1.0
TIME_STEP = 0.1
HALF_STEP = 0.05

FIELDS = 8
TINY = 1e-24
VISC_SCALE = 2.0 * VISCOSITY * SOUND_SPEED * SMOOTH
SOFTENING = 0.01 * SMOOTH * SMOOTH
REACH = 2.0 * SMOOTH


def exchange(tiles, axis, dim):
    count, length = lax.axis_size(axis), tiles.shape[dim]
    last = lax.slice_in_dim(tiles, length - 1, length, axis=dim)
    first = lax.slice_in_dim(tiles, 0, 1, axis=dim)
    at = lax.axis_index(axis)
    if count == 1:
        before = after = jnp.zeros_like(first)
    elif count == 2:
        got = lax.ppermute(jnp.where(at == 0, last, first), axis, [(0, 1), (1, 0)])
        before = jnp.where(at == 0, 0.0, got)
        after = jnp.where(at == 0, got, 0.0)
    else:
        before = lax.ppermute(last, axis, [(i, (i + 1) % count) for i in range(count)])
        after = lax.ppermute(first, axis, [(i, (i - 1) % count) for i in range(count)])
        before = jnp.where(at == 0, 0.0, before)
        after = jnp.where(at == count - 1, 0.0, after)
    return jnp.concatenate([before, tiles, after], axis=dim)


def with_halo(tiles):
    for axis, dim in (("gy", 1), ("gz", 2), ("gx", 0)):
        tiles = exchange(tiles, axis, dim)
    return tiles


def split3(values):
    high = values.astype(jnp.bfloat16).astype(jnp.float32)
    left = values - high
    middle = left.astype(jnp.bfloat16).astype(jnp.float32)
    return high, middle, left - middle


def split2(values):
    high = values.astype(jnp.bfloat16).astype(jnp.float32)
    return high, (values - high).astype(jnp.bfloat16).astype(jnp.float32)


def squares(tile):
    product = tile * tile
    mixed = tile[0:3] * tile[3:6]
    return product[0:1] + product[1:2] + product[2:3], mixed[0:1] + mixed[1:2] + mixed[2:3]


def near_side(tile):
    high, middle = split2(tile)
    square, mixed = squares(high + middle)
    extra = jnp.concatenate([square, mixed] + [jnp.zeros_like(square)] * 6, 0)
    row = lax.broadcasted_iota(jnp.int32, extra.shape, 0)
    extra_high, extra_middle, extra_low = split3(extra)
    extra_high = jnp.where((row >= 2) & (row < 5), 1.0, extra_high)
    pieces = [high, middle, high, middle, extra_high, extra_middle, extra_low, jnp.zeros_like(tile)]
    return jnp.concatenate(pieces, 0).astype(jnp.bfloat16)


ONES_ROW = 4 * FIELDS + 2
DEPTH = 8 * FIELDS


def own_side(tile):
    high, middle = split2(tile)
    square, mixed = squares(high + middle)
    zero, one = jnp.zeros_like(square), jnp.ones_like(square)
    sides = []
    for order, value, marks in (
        (lambda t: jnp.concatenate([-2.0 * t[0:3]] + [zero] * 5, 0), square, [one, zero]),
        (lambda t: -jnp.concatenate([t[3:6], t[0:3], zero, zero], 0), mixed, [zero, one]),
    ):
        rest = jnp.concatenate(marks + [zero] * 6, 0)
        first = jnp.concatenate(marks + list(split3(value)) + [zero] * 3, 0)
        pieces = [order(high)] * 2 + [order(middle)] * 2 + [first, rest, rest]
        pieces += [jnp.zeros_like(tile)] * (16 - len(pieces))
        sides.append(jnp.transpose(jnp.concatenate(pieces, 0)))
    return jnp.concatenate(sides, 0).astype(jnp.bfloat16)


def pressure_rows(tile):
    rho, mass = tile[6:7], tile[7:8]
    safe = jnp.where(mass > 0, rho, 1.0)
    square = safe * safe
    return safe * (1.0 / VISC_SCALE), STIFFNESS * (square * square * square * safe - 1.0) / square


def count_cells(halo_ref, counts):
    for x in range(halo_ref.shape[0]):
        for y in range(halo_ref.shape[1]):
            live = (halo_ref[x, y, :, 7] > 0).astype(jnp.float32)
            column = jnp.sum(live, axis=1, keepdims=True).astype(jnp.int32)
            for z in range(halo_ref.shape[2]):
                counts[x, y, z] = column[z, 0]


def compact(halo_ref, counts, near, blocks, cells):
    lane = lax.broadcasted_iota(jnp.int32, (FIELDS, 128), 1)
    row = lax.broadcasted_iota(jnp.int32, (FIELDS, 128), 0)
    places = all_cells(cells)
    at = [jnp.int32(0)] * len(places)
    for sx in range(3):
        for sy in range(3):
            for sz in range(3):
                shift = jnp.where(row == 0, sx - 1.5, jnp.where(row == 1, sy - 1.5, jnp.where(row == 2, sz - 1.5, 0.0)))
                for c, (cx, cy, cz) in enumerate(places):
                    block, inside = lax.shift_right_logical(at[c], 7), at[c] & 127
                    rolled = pltpu.roll(halo_ref[cx + sx, cy + sy, cz + sz] + shift, inside, axis=1)
                    pltpu.store(near.at[c, block], rolled, mask=lane >= inside)
                    near[c, block + 1] = rolled
                    at[c] = at[c] + counts[cx + sx, cy + sy, cz + sz]
    for c in range(len(places)):
        block, inside = lax.shift_right_logical(at[c], 7), at[c] & 127
        zeros = jnp.zeros((FIELDS, 128), jnp.float32)
        pltpu.store(near.at[c, block], zeros, mask=lane >= inside)
        near[c, block + 1] = zeros
        blocks[c] = lax.shift_right_logical(at[c] + 255, 8)


def pair_sums(halo_ref, counts, near, blocks, own, terms, slots, pushed, rated, cell, index):
    cx, cy, cz = cell
    row = lax.broadcasted_iota(jnp.int32, (FIELDS, 128), 0)
    tile = halo_ref[cx + 1, cy + 1, cz + 1] - jnp.where(row < 3, 0.5, 0.0)
    own[...] = own_side(tile)
    columns = jnp.transpose(jnp.concatenate(list(pressure_rows(tile)) + [jnp.zeros((6, 128), jnp.float32)], 0))
    for k in range(2):
        terms[k] = jnp.broadcast_to(columns[:, k : k + 1], (128, 128))
    pushed[index] = jnp.zeros(pushed.shape[1:], jnp.float32)
    rated[index] = jnp.zeros(rated.shape[1:], jnp.float32)
    here = counts[cx + 1, cy + 1, cz + 1]
    chunks = lax.shift_right_logical(here + 15, 4)
    count = blocks[index]
    for ref in slots[1][1:3]:
        ref[...] = jnp.zeros(ref.shape, ref.dtype)

    def run(rows):
        def products(block, slot):
            pairs, right, _, listed_terms = slot
            tiles = [near[index, 2 * block + side] for side in range(2)]
            sides = jnp.concatenate([near_side(tile) for tile in tiles], 1)
            for side, tile in enumerate(tiles):
                for k, value in enumerate((*pressure_rows(tile), GRADIENT * tile[7:8])):
                    listed_terms[side, k : k + 1] = value
            made = []
            for k in range(2):
                right[:, pl.ds(256 * k, 256)] = sides
                made.append(jnp.dot(own[pl.ds(128 * k, rows), 0:DEPTH], sides, preferred_element_type=jnp.float32))
            for part in range(rows // 8):
                at = pl.ds(8 * part, 8)
                dist_sq = jnp.maximum(made[0][8 * part : 8 * part + 8], TINY)
                dist = dist_sq * lax.rsqrt(dist_sq)
                fall = jnp.maximum(1.0 - (dist if REACH == 1.0 else dist * (1.0 / REACH)), 0.0)
                pairs[0, at] = fall
                pairs[1, at] = made[1][8 * part : 8 * part + 8]
                pairs[2, at] = dist_sq + SOFTENING

        def add(slot):
            pairs, _, push_parts, listed_terms = slot
            js = [[jnp.broadcast_to(listed_terms[side, k : k + 1], (8, 128)) for k in range(3)] for side in range(2)]
            for part in range(rows // 16):
                pushes = []
                for half in range(2):
                    at = pl.ds(16 * part + 8 * half, 8)
                    qi, ai = terms[0, at], terms[1, at]
                    rate = rated[index, at]
                    line = []
                    for side, (qj, aj, mj) in enumerate(js):
                        lanes = pl.ds(128 * side, 128)
                        fall, along, soft_sq = [pairs[k, at, lanes] for k in range(3)]
                        weight = fall * fall * fall * mj
                        viscous = jnp.minimum(along, 0.0) / (soft_sq * (qi + qj))
                        line.append(weight * (ai + aj - viscous))
                        rate += weight * along
                    rated[index, at] = rate
                    pushes.append(jnp.concatenate(line, 1))
                push = jnp.concatenate(pushes, 0)
                high = push.astype(jnp.bfloat16)
                push_parts[pl.ds(16 * part, 16), 0:256] = high
                push_parts[pl.ds(16 * part, 16), 256:512] = (push - high.astype(jnp.float32)).astype(jnp.bfloat16)

        def reduce(slot):
            _, right, push_parts, _ = slot
            pushed[index, 0:rows, 0:DEPTH] += lax.dot_general(
                push_parts[0:rows], right[...], (((1,), (1,)), ((), ())), preferred_element_type=jnp.float32
            )

        products(0, slots[0])

        def step(pair, carry):
            reduce(slots[1])
            products(2 * pair + 1, slots[1])
            add(slots[0])
            reduce(slots[0])
            products(2 * pair + 2, slots[0])
            add(slots[1])
            return carry

        lax.fori_loop(0, lax.shift_right_logical(count, 1), step, 0)
        reduce(slots[1])

        @pl.when((count & 1) == 1)
        def _():
            add(slots[0])
            reduce(slots[0])

    for rows in range(16, 129, 16):
        pl.when(chunks == rows // 16)(functools.partial(run, rows))


def over_cells(halo_ref, scratch, cells, visit):
    counts, blocks, near, own, terms, pushed, rated = scratch[:7]
    slots = (scratch[7:11], scratch[11:15])
    count_cells(halo_ref, counts)
    compact(halo_ref, counts, near, blocks, cells)

    def one(index, carry):
        cz = index % cells[2]
        cy = lax.div(index, cells[2]) % cells[1]
        cx = lax.div(index, cells[1] * cells[2])
        pair_sums(halo_ref, counts, near, blocks, own, terms, slots, pushed, rated, (cx, cy, cz), index)
        return carry

    lax.fori_loop(0, cells[0] * cells[1] * cells[2], one, 0)
    lane = lax.broadcasted_iota(jnp.int32, (1, 128), 1)
    for index, (cx, cy, cz) in enumerate(all_cells(cells)):
        rows = jnp.transpose(pushed[index])
        tile = halo_ref[cx + 1, cy + 1, cz + 1]
        live = lane < counts[cx + 1, cy + 1, cz + 1]
        place = sum(split2(tile[0:3] - 0.5))
        total = rows[0:3] + rows[FIELDS : FIELDS + 3]
        accel = jnp.where(live, place * rows[ONES_ROW : ONES_ROW + 1] - total, 0.0)
        accel = [accel[0:1], accel[1:2], accel[2:3] - GRAVITY]
        rate = jnp.sum(jnp.transpose(rated[index]), axis=0, keepdims=True)
        visit(cx, cy, cz, accel, jnp.where(live, -rate, 0.0))


def scratch_for(halo_shape, cells):
    own = cells[0] * cells[1] * cells[2]
    slot = [
        pltpu.VMEM((3, 128, 256), jnp.float32),
        pltpu.VMEM((DEPTH, 512), jnp.bfloat16),
        pltpu.VMEM((128, 512), jnp.bfloat16),
        pltpu.VMEM((2, FIELDS, 128), jnp.float32),
    ]
    return [
        pltpu.SMEM(halo_shape[:3], jnp.int32),
        pltpu.SMEM((own,), jnp.int32),
        pltpu.VMEM((own, 32, FIELDS, 128), jnp.float32),
        pltpu.VMEM((256, 128), jnp.bfloat16),
        pltpu.VMEM((2, 128, 128), jnp.float32),
        pltpu.VMEM((own, 128, 128), jnp.float32),
        pltpu.VMEM((own, 128, 128), jnp.float32),
        *slot,
        *slot,
    ]


def call(kernel, cells, outs, args, scratch=(), scalars=(), grant=16):
    whole = pl.BlockSpec(memory_space=pltpu.VMEM)
    table = pl.BlockSpec(memory_space=pltpu.SMEM)
    return pl.pallas_call(
        functools.partial(kernel, cells),
        out_shape=[out if hasattr(out, "dtype") else jax.ShapeDtypeStruct(out, jnp.float32) for out in outs],
        in_specs=[whole] * len(args) + [table] * len(scalars),
        out_specs=[whole] * len(outs),
        scratch_shapes=list(scratch),
        compiler_params=pltpu.CompilerParams(vmem_limit_bytes=grant * 1024 * 1024),
    )(*args, *scalars)


def all_cells(cells):
    return [(x, y, z) for x in range(cells[0]) for y in range(cells[1]) for z in range(cells[2])]


def state_kernel(
    cells, offsets_ref, velocity_ref, density_ref, mass_ref, direction_ref, slot_ref, occupancy_ref, state_ref, target_ref
):
    lane = lax.broadcasted_iota(jnp.int32, (1, 128), 1)
    for cx, cy, cz in all_cells(cells):
        here = pl.ds(cz, 1)
        for k in range(3):
            state_ref[cx, cy, cz, k : k + 1] = offsets_ref[k, cx, cy, here]
            state_ref[cx, cy, cz, k + 3 : k + 4] = velocity_ref[k, cx, cy, here]
        state_ref[cx, cy, cz, 6:7] = density_ref[cx, cy, here]
        live = lane < occupancy_ref[cx, cy, cz]
        state_ref[cx, cy, cz, 7:8] = jnp.where(live, mass_ref[cx, cy, here], 0.0)
        way, slot = direction_ref[cx, cy, here], slot_ref[cx, cy, here]
        target = jnp.where(way == 1, slot, jnp.where(way == 2, slot + MOVES, -1))
        target_ref[cx, cy, here] = jnp.where(live, target, -2)


def half_kernel(cells, halo_ref, half_ref, *scratch):
    def visit(cx, cy, cz, accel, rate):
        tile = halo_ref[cx + 1, cy + 1, cz + 1]
        change = jnp.concatenate([tile[3:6]] + accel + [rate, jnp.zeros_like(rate)], 0)
        half_ref[cx, cy, cz] = tile + HALF_STEP * change

    over_cells(halo_ref, scratch, cells, visit)


def last_kernel(
    cells, halo_ref, state_ref, target_ref, lower_ref, upper_ref, position_ref, velocity_ref, density_ref, *scratch
):
    slots = lax.broadcasted_iota(jnp.int32, (2 * MOVES, 128), 0)
    row = lax.broadcasted_iota(jnp.int32, (FIELDS, 128), 0)
    lists = [jnp.zeros((FIELDS, 2 * MOVES), jnp.float32)]

    def visit(cx, cy, cz, accel, rate):
        tile = state_ref[cx, cy, cz]
        half = halo_ref[cx + 1, cy + 1, cz + 1]
        change = jnp.concatenate([half[3:6]] + accel + [rate, jnp.zeros_like(rate)], 0)
        new = tile + TIME_STEP * change
        here = pl.ds(cz, 1)
        target = target_ref[cx, cy, here]
        kept = jnp.where(target == -1, new, 0.0)
        for k in range(3):
            position_ref[k, cx, cy, here] = kept[k : k + 1]
            velocity_ref[k, cx, cy, here] = kept[k + 3 : k + 4]
        density_ref[cx, cy, here] = kept[6:7]
        chosen = (slots == target).astype(jnp.float32).astype(jnp.bfloat16)
        place = jnp.where(row == 0, float(cx), jnp.where(row == 1, float(cy), jnp.where(row == 2, float(cz), 0.0)))
        record = jnp.where(row == 7, 1.0, new + place)
        for piece in split3(record):
            lists[0] += lax.dot_general(
                piece.astype(jnp.bfloat16), chosen, (((1,), (1,)), ((), ())), preferred_element_type=jnp.float32
            )

    over_cells(halo_ref, scratch, cells, visit)
    for side, (out_ref, moved) in enumerate(((lower_ref, -float(cells[0])), (upper_ref, float(cells[0])))):
        half = lists[0][:, MOVES * side : MOVES * (side + 1)]
        out_ref[...] = half + jnp.where(row == 0, moved, 0.0) * half[7:8]


def body(offsets, velocity, density, mass, occupancy, move_direction, move_slot):
    cells = density.shape[:3]
    tiles = (*cells, FIELDS, 128)
    fields = (offsets, velocity, density, mass, move_direction, move_slot)
    places = jax.ShapeDtypeStruct(density.shape, jnp.int32)
    state, target = call(state_kernel, cells, [tiles, places], fields, scalars=(occupancy,), grant=60)
    halo = with_halo(state)
    scratch = scratch_for(halo.shape, cells)
    (half,) = call(half_kernel, cells, [tiles], (halo,), scratch)
    outs = [(FIELDS, MOVES), (FIELDS, MOVES), offsets.shape, velocity.shape, density.shape]
    lower, upper, position_next, velocity_next, density_next = call(
        last_kernel, cells, outs, (with_halo(half), state, target), scratch
    )
    count, at = lax.axis_size("gx"), lax.axis_index("gx")
    if count > 1:
        lower = lax.ppermute(lower, "gx", [(i, (i + 1) % count) for i in range(count)])
        upper = lax.ppermute(upper, "gx", [(i, (i - 1) % count) for i in range(count)])
    lists = jnp.stack([jnp.where(at == 0, 0.0, lower), jnp.where(at == count - 1, 0.0, upper)], 1)
    arrivals = lists[:7].reshape(7, 2, 1, 1, 1, MOVES)
    return (position_next, velocity_next, density_next, arrivals)


def solution(mesh):
    placed = (
        P(None, "gx", "gy", "gz", None),
        P(None, "gx", "gy", "gz", None),
        P("gx", "gy", "gz", None),
        P("gx", "gy", "gz", None),
        P("gx", "gy", "gz"),
        P("gx", "gy", "gz", None),
        P("gx", "gy", "gz", None),
    )
    return jax.shard_map(
        body,
        mesh=mesh,
        in_specs=placed,
        out_specs=(
            P(None, "gx", "gy", "gz", None),
            P(None, "gx", "gy", "gz", None),
            P("gx", "gy", "gz", None),
            P(None, None, "gx", "gy", "gz", None),
        ),
        check_vma=False,
    )
```

```python
import functools
import math

import jax
import jax.numpy as jnp
from jax import lax
from jax.experimental import pallas as pl
from jax.experimental.pallas import tpu as pltpu
from jax.sharding import PartitionSpec as P

MOVES = 128

SMOOTH = 0.5
KERNEL_NORM = 21.0 / (16.0 * math.pi * SMOOTH**3)
GRADIENT = 5.0 * KERNEL_NORM / SMOOTH**2
SOUND_SPEED = 10.0
STIFFNESS = SOUND_SPEED**2 / 7.0
VISCOSITY = 0.1
GRAVITY = 1.0
TIME_STEP = 0.1
HALF_STEP = 0.05

FIELDS = 8
TINY = 1e-24
VISC_SCALE = 2.0 * VISCOSITY * SOUND_SPEED * SMOOTH
SOFTENING = 0.01 * SMOOTH * SMOOTH
REACH = 2.0 * SMOOTH


def exchange(tiles, axis, dim):
    count, length = lax.axis_size(axis), tiles.shape[dim]
    last = lax.slice_in_dim(tiles, length - 1, length, axis=dim)
    first = lax.slice_in_dim(tiles, 0, 1, axis=dim)
    at = lax.axis_index(axis)
    if count == 1:
        before = after = jnp.zeros_like(first)
    elif count == 2:
        got = lax.ppermute(jnp.where(at == 0, last, first), axis, [(0, 1), (1, 0)])
        before = jnp.where(at == 0, 0.0, got)
        after = jnp.where(at == 0, got, 0.0)
    else:
        before = lax.ppermute(last, axis, [(i, (i + 1) % count) for i in range(count)])
        after = lax.ppermute(first, axis, [(i, (i - 1) % count) for i in range(count)])
        before = jnp.where(at == 0, 0.0, before)
        after = jnp.where(at == count - 1, 0.0, after)
    return jnp.concatenate([before, tiles, after], axis=dim)


def with_halo(tiles):
    for axis, dim in (("gy", 1), ("gz", 2), ("gx", 0)):
        tiles = exchange(tiles, axis, dim)
    return tiles


def split3(values):
    high = values.astype(jnp.bfloat16).astype(jnp.float32)
    left = values - high
    middle = left.astype(jnp.bfloat16).astype(jnp.float32)
    return high, middle, left - middle


def split2(values):
    high = values.astype(jnp.bfloat16).astype(jnp.float32)
    return high, (values - high).astype(jnp.bfloat16).astype(jnp.float32)


def squares(tile):
    product = tile * tile
    mixed = tile[0:3] * tile[3:6]
    return product[0:1] + product[1:2] + product[2:3], mixed[0:1] + mixed[1:2] + mixed[2:3]


def near_side(high, middle):
    square, mixed = squares(high + middle)
    extra = jnp.concatenate([square, mixed] + [jnp.zeros_like(square)] * 6, 0)
    row = lax.broadcasted_iota(jnp.int32, extra.shape, 0)
    extra_high, extra_middle, extra_low = split3(extra)
    extra_high = jnp.where((row >= 2) & (row < 5), 1.0, extra_high)
    pieces = [high, middle, high, middle, extra_high, extra_middle, extra_low, jnp.zeros_like(high)]
    return jnp.concatenate(pieces, 0).astype(jnp.bfloat16)


DEPTH = 8 * FIELDS


def own_side(tile):
    high, middle = split2(tile)
    square, mixed = squares(high + middle)
    zero, one = jnp.zeros_like(square), jnp.ones_like(square)
    sides = []
    for order, value, marks in (
        (lambda t: jnp.concatenate([-2.0 * t[0:3]] + [zero] * 5, 0), square, [one, zero]),
        (lambda t: -jnp.concatenate([t[3:6], t[0:3], zero, zero], 0), mixed, [zero, one]),
    ):
        rest = jnp.concatenate(marks + [zero] * 6, 0)
        first = jnp.concatenate(marks + list(split3(value)) + [zero] * 3, 0)
        pieces = [order(high)] * 2 + [order(middle)] * 2 + [first, rest, rest]
        pieces += [jnp.zeros_like(tile)] * (16 - len(pieces))
        sides.append(jnp.transpose(jnp.concatenate(pieces, 0)))
    return jnp.concatenate(sides, 0).astype(jnp.bfloat16)


def pressure_rows(tile):
    rho, mass = tile[6:7], tile[7:8]
    safe = jnp.where(mass > 0, rho, 1.0)
    square = safe * safe
    return safe * (1.0 / VISC_SCALE), STIFFNESS * (square * square * square * safe - 1.0) / square


def count_cells(halo_ref, counts):
    for x in range(halo_ref.shape[0]):
        for y in range(halo_ref.shape[1]):
            live = (halo_ref[x, y, :, 7] > 0).astype(jnp.float32)
            column = jnp.sum(live, axis=1, keepdims=True).astype(jnp.int32)
            for z in range(halo_ref.shape[2]):
                counts[x, y, z] = column[z, 0]


def compact(halo_ref, counts, near, blocks, cells):
    lane = lax.broadcasted_iota(jnp.int32, (FIELDS, 128), 1)
    row = lax.broadcasted_iota(jnp.int32, (FIELDS, 128), 0)
    places = all_cells(cells)
    at = [jnp.int32(0)] * len(places)
    for sx in range(3):
        for sy in range(3):
            for sz in range(3):
                shift = jnp.where(row == 0, sx - 1.5, jnp.where(row == 1, sy - 1.5, jnp.where(row == 2, sz - 1.5, 0.0)))
                for c, (cx, cy, cz) in enumerate(places):
                    block, inside = lax.shift_right_logical(at[c], 7), at[c] & 127
                    rolled = pltpu.roll(halo_ref[cx + sx, cy + sy, cz + sz] + shift, inside, axis=1)
                    pltpu.store(near.at[c, block], rolled, mask=lane >= inside)
                    near[c, block + 1] = rolled
                    at[c] = at[c] + counts[cx + sx, cy + sy, cz + sz]
    for c in range(len(places)):
        block, inside = lax.shift_right_logical(at[c], 7), at[c] & 127
        zeros = jnp.zeros((FIELDS, 128), jnp.float32)
        pltpu.store(near.at[c, block], zeros, mask=lane >= inside)
        near[c, block + 1] = zeros
        blocks[c] = lax.shift_right_logical(at[c] + 255, 8)


def pair_sums(halo_ref, counts, near, blocks, own, terms, slots, total, cell, index):
    cx, cy, cz = cell
    row = lax.broadcasted_iota(jnp.int32, (FIELDS, 128), 0)
    tile = halo_ref[cx + 1, cy + 1, cz + 1] - jnp.where(row < 3, 0.5, 0.0)
    own[...] = own_side(tile)
    columns = jnp.transpose(jnp.concatenate(list(pressure_rows(tile)) + [jnp.zeros((6, 128), jnp.float32)], 0))
    for k in range(2):
        terms[k] = jnp.broadcast_to(columns[:, k : k + 1], (128, 128))
    total[index] = jnp.zeros(total.shape[1:], jnp.float32)
    here = counts[cx + 1, cy + 1, cz + 1]
    chunks = lax.shift_right_logical(here + 15, 4)
    count = blocks[index]

    def run(rows):
        def products(block, slot):
            pairs, listed = slot
            sides = []
            for side in range(2):
                tile = near[index, 2 * block + side]
                high, middle = split2(tile)
                sides.append(near_side(high, middle))
                listed[side, 0:3] = high[0:3] + middle[0:3]
                for k, value in enumerate((*pressure_rows(tile), GRADIENT * tile[7:8])):
                    listed[side, 3 + k : 4 + k] = value
            right = jnp.concatenate(sides, 1)
            for k in range(2):
                pairs[k, 0:rows] = jnp.dot(own[pl.ds(128 * k, rows), 0:DEPTH], right, preferred_element_type=jnp.float32)

        def add(slot):
            pairs, listed = slot
            js = [[jnp.broadcast_to(listed[side, k : k + 1], (8, 128)) for k in range(6)] for side in range(2)]
            for part in range(rows // 8):
                at = pl.ds(8 * part, 8)
                qi, ai = terms[0, at], terms[1, at]
                sums = [total[index, k, at] for k in range(5)]
                for side, (xj, yj, zj, qj, aj, mj) in enumerate(js):
                    lanes = pl.ds(128 * side, 128)
                    dist_sq, along = jnp.maximum(pairs[0, at, lanes], TINY), pairs[1, at, lanes]
                    dist = dist_sq * lax.rsqrt(dist_sq)
                    fall = jnp.maximum(1.0 - (dist if REACH == 1.0 else dist * (1.0 / REACH)), 0.0)
                    weight = fall * fall * fall * mj
                    viscous = jnp.minimum(along, 0.0) / ((dist_sq + SOFTENING) * (qi + qj))
                    push = weight * (ai + aj - viscous)
                    sums[0] += push
                    sums[1] += push * xj
                    sums[2] += push * yj
                    sums[3] += push * zj
                    sums[4] += weight * along
                for k in range(5):
                    total[index, k, at] = sums[k]

        products(0, slots[0])

        def step(pair, carry):
            products(2 * pair + 1, slots[1])
            add(slots[0])
            products(2 * pair + 2, slots[0])
            add(slots[1])
            return carry

        lax.fori_loop(0, lax.shift_right_logical(count, 1), step, 0)
        pl.when((count & 1) == 1)(lambda: add(slots[0]))

    for rows in range(16, 129, 16):
        pl.when(chunks == rows // 16)(functools.partial(run, rows))


def over_cells(halo_ref, scratch, cells, visit):
    counts, blocks, near, own, terms, total = scratch[:6]
    count_cells(halo_ref, counts)
    compact(halo_ref, counts, near, blocks, cells)

    def one(index, carry):
        cz = index % cells[2]
        cy = lax.div(index, cells[2]) % cells[1]
        cx = lax.div(index, cells[1] * cells[2])
        pair_sums(halo_ref, counts, near, blocks, own, terms, (scratch[6:8], scratch[8:10]), total, (cx, cy, cz), index)
        return carry

    lax.fori_loop(0, cells[0] * cells[1] * cells[2], one, 0)
    ones = jnp.ones((16, 128), jnp.bfloat16)
    lane = lax.broadcasted_iota(jnp.int32, (1, 128), 1)
    for index in range(cells[0] * cells[1] * cells[2]):
        cx, cy, cz = index // (cells[1] * cells[2]), index // cells[2] % cells[1], index % cells[2]
        flat = total[index].reshape(5 * 128, 128)
        high = flat.astype(jnp.bfloat16)
        left = flat - high.astype(jnp.float32)
        middle = left.astype(jnp.bfloat16)
        summed = sum(
            lax.dot_general(ones, piece, (((1,), (1,)), ((), ())), preferred_element_type=jnp.float32)[0:1]
            for piece in (high, middle)
        )
        sums = [summed[:, 128 * k : 128 * (k + 1)] for k in range(5)]
        tile = halo_ref[cx + 1, cy + 1, cz + 1]
        live = lane < counts[cx + 1, cy + 1, cz + 1]
        place = sum(split2(tile[0:3] - 0.5))
        accel = [jnp.where(live, place[k : k + 1] * sums[0] - sums[k + 1], 0.0) for k in range(3)]
        accel[2] = accel[2] - GRAVITY
        visit(cx, cy, cz, accel, jnp.where(live, -sums[4], 0.0))


def scratch_for(halo_shape, cells):
    own = cells[0] * cells[1] * cells[2]
    slot = [pltpu.VMEM((2, 128, 256), jnp.float32), pltpu.VMEM((2, FIELDS, 128), jnp.float32)]
    return [
        pltpu.SMEM(halo_shape[:3], jnp.int32),
        pltpu.SMEM((own,), jnp.int32),
        pltpu.VMEM((own, 32, FIELDS, 128), jnp.float32),
        pltpu.VMEM((256, 128), jnp.bfloat16),
        pltpu.VMEM((2, 128, 128), jnp.float32),
        pltpu.VMEM((own, 5, 128, 128), jnp.float32),
        *slot,
        *slot,
    ]


def call(kernel, cells, outs, args, scratch=(), source=pltpu.VMEM):
    whole = pl.BlockSpec(memory_space=pltpu.VMEM)
    return pl.pallas_call(
        functools.partial(kernel, cells),
        out_shape=[out if hasattr(out, "dtype") else jax.ShapeDtypeStruct(out, jnp.float32) for out in outs],
        in_specs=[pl.BlockSpec(memory_space=source)] * len(args),
        out_specs=[whole] * len(outs),
        scratch_shapes=list(scratch),
        compiler_params=pltpu.CompilerParams(vmem_limit_bytes=16 * 1024 * 1024),
    )(*args)


def all_cells(cells):
    return [(x, y, z) for x in range(cells[0]) for y in range(cells[1]) for z in range(cells[2])]


def state_kernel(cells, *refs):
    sources, (state_ref, target_ref), copies, arrived = refs[:7], refs[7:9], refs[9:16], refs[16]
    moves = [pltpu.make_async_copy(sources[k], copies[k], arrived.at[k]) for k in range(len(sources))]
    for move in moves:
        move.start()
    for move in moves:
        move.wait()
    offsets_ref, velocity_ref, density_ref, mass_ref, direction_ref, slot_ref, occupancy_ref = copies
    lane = lax.broadcasted_iota(jnp.int32, (1, 128), 1)
    for cx, cy, cz in all_cells(cells):
        here = pl.ds(cz, 1)
        for k in range(3):
            state_ref[cx, cy, cz, k : k + 1] = offsets_ref[k, cx, cy, here]
            state_ref[cx, cy, cz, k + 3 : k + 4] = velocity_ref[k, cx, cy, here]
        state_ref[cx, cy, cz, 6:7] = density_ref[cx, cy, here]
        live = lane < occupancy_ref[cx, cy, cz]
        state_ref[cx, cy, cz, 7:8] = jnp.where(live, mass_ref[cx, cy, here], 0.0)
        way, slot = direction_ref[cx, cy, here], slot_ref[cx, cy, here]
        target = jnp.where(way == 1, slot, jnp.where(way == 2, slot + MOVES, -1))
        target_ref[cx, cy, here] = jnp.where(live, target, -2)


def half_kernel(cells, halo_ref, half_ref, *scratch):
    def visit(cx, cy, cz, accel, rate):
        tile = halo_ref[cx + 1, cy + 1, cz + 1]
        change = jnp.concatenate([tile[3:6]] + accel + [rate, jnp.zeros_like(rate)], 0)
        half_ref[cx, cy, cz] = tile + HALF_STEP * change

    over_cells(halo_ref, scratch, cells, visit)


def last_kernel(
    cells, halo_ref, state_ref, target_ref, lower_ref, upper_ref, position_ref, velocity_ref, density_ref, *scratch
):
    slots = lax.broadcasted_iota(jnp.int32, (2 * MOVES, 128), 0)
    row = lax.broadcasted_iota(jnp.int32, (FIELDS, 128), 0)
    lists = [jnp.zeros((FIELDS, 2 * MOVES), jnp.float32)]

    def visit(cx, cy, cz, accel, rate):
        tile = state_ref[cx, cy, cz]
        half = halo_ref[cx + 1, cy + 1, cz + 1]
        change = jnp.concatenate([half[3:6]] + accel + [rate, jnp.zeros_like(rate)], 0)
        new = tile + TIME_STEP * change
        here = pl.ds(cz, 1)
        target = target_ref[cx, cy, here]
        kept = jnp.where(target == -1, new, 0.0)
        for k in range(3):
            position_ref[k, cx, cy, here] = kept[k : k + 1]
            velocity_ref[k, cx, cy, here] = kept[k + 3 : k + 4]
        density_ref[cx, cy, here] = kept[6:7]
        chosen = (slots == target).astype(jnp.float32).astype(jnp.bfloat16)
        place = jnp.where(row == 0, float(cx), jnp.where(row == 1, float(cy), jnp.where(row == 2, float(cz), 0.0)))
        record = jnp.where(row == 7, 1.0, new + place)
        for piece in split3(record):
            lists[0] += lax.dot_general(
                piece.astype(jnp.bfloat16), chosen, (((1,), (1,)), ((), ())), preferred_element_type=jnp.float32
            )

    over_cells(halo_ref, scratch, cells, visit)
    for side, (out_ref, moved) in enumerate(((lower_ref, -float(cells[0])), (upper_ref, float(cells[0])))):
        half = lists[0][:, MOVES * side : MOVES * (side + 1)]
        out_ref[...] = half + jnp.where(row == 0, moved, 0.0) * half[7:8]


def body(offsets, velocity, density, mass, occupancy, move_direction, move_slot):
    cells = density.shape[:3]
    tiles = (*cells, FIELDS, 128)
    fields = (offsets, velocity, density, mass, move_direction, move_slot, occupancy)
    places = jax.ShapeDtypeStruct(density.shape, jnp.int32)
    fields = tuple(pltpu.with_memory_space_constraint(field, pltpu.HBM) for field in fields)
    staged = [pltpu.VMEM(field.shape, field.dtype) for field in fields[:-1]]
    staged += [pltpu.SMEM(occupancy.shape, occupancy.dtype), pltpu.SemaphoreType.DMA((len(fields),))]
    state, target = call(state_kernel, cells, [tiles, places], fields, staged, source=pltpu.HBM)
    halo = with_halo(state)
    scratch = scratch_for(halo.shape, cells)
    (half,) = call(half_kernel, cells, [tiles], (halo,), scratch)
    outs = [(FIELDS, MOVES), (FIELDS, MOVES), offsets.shape, velocity.shape, density.shape]
    lower, upper, position_next, velocity_next, density_next = call(
        last_kernel, cells, outs, (with_halo(half), state, target), scratch
    )
    count, at = lax.axis_size("gx"), lax.axis_index("gx")
    if count > 1:
        lower = lax.ppermute(lower, "gx", [(i, (i + 1) % count) for i in range(count)])
        upper = lax.ppermute(upper, "gx", [(i, (i - 1) % count) for i in range(count)])
    lists = jnp.stack([jnp.where(at == 0, 0.0, lower), jnp.where(at == count - 1, 0.0, upper)], 1)
    arrivals = lists[:7].reshape(7, 2, 1, 1, 1, MOVES)
    return (position_next, velocity_next, density_next, arrivals)


def solution(mesh):
    placed = (
        P(None, "gx", "gy", "gz", None),
        P(None, "gx", "gy", "gz", None),
        P("gx", "gy", "gz", None),
        P("gx", "gy", "gz", None),
        P("gx", "gy", "gz"),
        P("gx", "gy", "gz", None),
        P("gx", "gy", "gz", None),
    )
    return jax.shard_map(
        body,
        mesh=mesh,
        in_specs=placed,
        out_specs=(
            P(None, "gx", "gy", "gz", None),
            P(None, "gx", "gy", "gz", None),
            P("gx", "gy", "gz", None),
            P(None, None, "gx", "gy", "gz", None),
        ),
        check_vma=False,
    )
```

```python
import functools
import math

import jax
import jax.numpy as jnp
from jax import lax
from jax.experimental import pallas as pl
from jax.experimental.pallas import tpu as pltpu
from jax.sharding import PartitionSpec as P


MOVES = 128

SMOOTH = 0.5
KERNEL_NORM = 21.0 / (16.0 * math.pi * SMOOTH**3)
GRADIENT = 5.0 * KERNEL_NORM / SMOOTH**2
SOUND_SPEED = 10.0
STIFFNESS = SOUND_SPEED**2 / 7.0
VISCOSITY = 0.1
GRAVITY = 1.0
TIME_STEP = 0.1
HALF_STEP = 0.05

FIELDS = 8
TINY = 1e-24
VISC_SCALE = 2.0 * VISCOSITY * SOUND_SPEED * SMOOTH
SOFTENING = 0.01 * SMOOTH * SMOOTH
REACH = 2.0 * SMOOTH


def exchange(tiles, axis, dim):
    count, length = lax.axis_size(axis), tiles.shape[dim]
    last = lax.slice_in_dim(tiles, length - 1, length, axis=dim)
    first = lax.slice_in_dim(tiles, 0, 1, axis=dim)
    at = lax.axis_index(axis)
    if count == 1:
        before = after = jnp.zeros_like(first)
    elif count == 2:
        got = lax.ppermute(jnp.where(at == 0, last, first), axis, [(0, 1), (1, 0)])
        before = jnp.where(at == 0, 0.0, got)
        after = jnp.where(at == 0, got, 0.0)
    else:
        before = lax.ppermute(last, axis, [(i, (i + 1) % count) for i in range(count)])
        after = lax.ppermute(first, axis, [(i, (i - 1) % count) for i in range(count)])
        before = jnp.where(at == 0, 0.0, before)
        after = jnp.where(at == count - 1, 0.0, after)
    return jnp.concatenate([before, tiles, after], axis=dim)


def with_halo(tiles):
    for axis, dim in (("gy", 1), ("gz", 2), ("gx", 0)):
        tiles = exchange(tiles, axis, dim)
    return tiles


def split3(values):
    high = values.astype(jnp.bfloat16).astype(jnp.float32)
    left = values - high
    middle = left.astype(jnp.bfloat16).astype(jnp.float32)
    return high, middle, left - middle


def split2(values):
    high = values.astype(jnp.bfloat16).astype(jnp.float32)
    return high, (values - high).astype(jnp.bfloat16).astype(jnp.float32)


def squares(tile):
    product = tile * tile
    mixed = tile[0:3] * tile[3:6]
    return product[0:1] + product[1:2] + product[2:3], mixed[0:1] + mixed[1:2] + mixed[2:3]


def near_side(high, middle):
    square, mixed = squares(high + middle)
    extra = jnp.concatenate([square, mixed] + [jnp.zeros_like(square)] * 6, 0)
    row = lax.broadcasted_iota(jnp.int32, extra.shape, 0)
    extra_high, extra_middle, extra_low = split3(extra)
    extra_high = jnp.where((row >= 2) & (row < 5), 1.0, extra_high)
    pieces = [high, middle, high, middle, extra_high, extra_middle, extra_low, jnp.zeros_like(high)]
    return jnp.concatenate(pieces, 0).astype(jnp.bfloat16)


DEPTH = 8 * FIELDS


def own_side(tile):
    high, middle = split2(tile)
    square, mixed = squares(high + middle)
    zero, one = jnp.zeros_like(square), jnp.ones_like(square)
    sides = []
    for order, value, marks in (
        (lambda t: jnp.concatenate([-2.0 * t[0:3]] + [zero] * 5, 0), square, [one, zero]),
        (lambda t: -jnp.concatenate([t[3:6], t[0:3], zero, zero], 0), mixed, [zero, one]),
    ):
        rest = jnp.concatenate(marks + [zero] * 6, 0)
        first = jnp.concatenate(marks + list(split3(value)) + [zero] * 3, 0)
        pieces = [order(high)] * 2 + [order(middle)] * 2 + [first, rest, rest]
        pieces += [jnp.zeros_like(tile)] * (16 - len(pieces))
        sides.append(jnp.transpose(jnp.concatenate(pieces, 0)))
    return jnp.concatenate(sides, 0).astype(jnp.bfloat16)


def pressure_rows(tile):
    rho, mass = tile[6:7], tile[7:8]
    safe = jnp.where(mass > 0, rho, 1.0)
    square = safe * safe
    return safe * (1.0 / VISC_SCALE), STIFFNESS * (square * square * square * safe - 1.0) / square


def count_cells(halo_ref, counts):
    for x in range(halo_ref.shape[0]):
        for y in range(halo_ref.shape[1]):
            live = (halo_ref[x, y, :, 7] > 0).astype(jnp.float32)
            column = jnp.sum(live, axis=1, keepdims=True).astype(jnp.int32)
            for z in range(halo_ref.shape[2]):
                counts[x, y, z] = column[z, 0]


def compact(halo_ref, counts, near, blocks, cells):
    lane = lax.broadcasted_iota(jnp.int32, (FIELDS, 128), 1)
    row = lax.broadcasted_iota(jnp.int32, (FIELDS, 128), 0)
    places = all_cells(cells)
    at = [jnp.int32(0)] * len(places)
    for sx in range(3):
        for sy in range(3):
            for sz in range(3):
                shift = jnp.where(row == 0, sx - 1.5, jnp.where(row == 1, sy - 1.5, jnp.where(row == 2, sz - 1.5, 0.0)))
                for c, (cx, cy, cz) in enumerate(places):
                    block, inside = lax.shift_right_logical(at[c], 7), at[c] & 127
                    rolled = pltpu.roll(halo_ref[cx + sx, cy + sy, cz + sz] + shift, inside, axis=1)
                    pltpu.store(near.at[c, block], rolled, mask=lane >= inside)
                    near[c, block + 1] = rolled
                    at[c] = at[c] + counts[cx + sx, cy + sy, cz + sz]
    for c in range(len(places)):
        block, inside = lax.shift_right_logical(at[c], 7), at[c] & 127
        zeros = jnp.zeros((FIELDS, 128), jnp.float32)
        pltpu.store(near.at[c, block], zeros, mask=lane >= inside)
        near[c, block + 1] = zeros
        blocks[c] = lax.shift_right_logical(at[c] + 255, 8)


def own_kernel(cells, tiles_ref, own_ref, terms_ref):
    row = lax.broadcasted_iota(jnp.int32, (FIELDS, 128), 0)
    for index, place in enumerate(all_cells(cells)):
        tile = tiles_ref[place] - jnp.where(row < 3, 0.5, 0.0)
        own_ref[index] = own_side(tile)
        columns = jnp.transpose(jnp.concatenate(list(pressure_rows(tile)) + [jnp.zeros((6, 128), jnp.float32)], 0))
        for k in range(2):
            terms_ref[index, k] = jnp.broadcast_to(columns[:, k : k + 1], (128, 128))


def pair_sums(counts, near, blocks, own, terms, slots, total, cell, index):
    cx, cy, cz = cell
    total[index] = jnp.zeros(total.shape[1:], jnp.float32)
    here = counts[cx + 1, cy + 1, cz + 1]
    chunks = lax.shift_right_logical(here + 15, 4)
    count = blocks[index]

    def run(rows):
        def products(block, slot):
            pairs, listed = slot
            sides = []
            for side in range(2):
                tile = near[index, 2 * block + side]
                high, middle = split2(tile)
                sides.append(near_side(high, middle))
                listed[side, 0:3] = high[0:3] + middle[0:3]
                for k, value in enumerate((*pressure_rows(tile), GRADIENT * tile[7:8])):
                    listed[side, 3 + k : 4 + k] = value
            right = jnp.concatenate(sides, 1)
            for k in range(2):
                pairs[k, 0:rows] = jnp.dot(own[index, pl.ds(128 * k, rows), 0:DEPTH], right, preferred_element_type=jnp.float32)

        def add(slot):
            pairs, listed = slot
            js = [[jnp.broadcast_to(listed[side, k : k + 1], (8, 128)) for k in range(6)] for side in range(2)]
            for part in range(rows // 8):
                at = pl.ds(8 * part, 8)
                qi, ai = terms[index, 0, at], terms[index, 1, at]
                sums = [total[index, k, at] for k in range(5)]
                for side, (xj, yj, zj, qj, aj, mj) in enumerate(js):
                    lanes = pl.ds(128 * side, 128)
                    dist_sq, along = jnp.maximum(pairs[0, at, lanes], TINY), pairs[1, at, lanes]
                    dist = dist_sq * lax.rsqrt(dist_sq)
                    fall = jnp.maximum(1.0 - (dist if REACH == 1.0 else dist * (1.0 / REACH)), 0.0)
                    weight = fall * fall * fall * mj
                    viscous = jnp.minimum(along, 0.0) / ((dist_sq + SOFTENING) * (qi + qj))
                    push = weight * (ai + aj - viscous)
                    sums[0] += push
                    sums[1] += push * xj
                    sums[2] += push * yj
                    sums[3] += push * zj
                    sums[4] += weight * along
                for k in range(5):
                    total[index, k, at] = sums[k]

        products(0, slots[0])

        def step(pair, carry):
            products(2 * pair + 1, slots[1])
            add(slots[0])
            products(2 * pair + 2, slots[0])
            add(slots[1])
            return carry

        lax.fori_loop(0, lax.shift_right_logical(count, 1), step, 0)
        pl.when((count & 1) == 1)(lambda: add(slots[0]))

    for rows in range(16, 129, 16):
        pl.when(chunks == rows // 16)(functools.partial(run, rows))


def over_cells(halo_ref, own, terms, scratch, cells, visit):
    counts, blocks, near, total = scratch[:4]
    count_cells(halo_ref, counts)
    compact(halo_ref, counts, near, blocks, cells)

    def one(index, carry):
        cz = index % cells[2]
        cy = lax.div(index, cells[2]) % cells[1]
        cx = lax.div(index, cells[1] * cells[2])
        pair_sums(counts, near, blocks, own, terms, (scratch[4:6], scratch[6:8]), total, (cx, cy, cz), index)
        return carry

    lax.fori_loop(0, cells[0] * cells[1] * cells[2], one, 0)
    ones = jnp.ones((16, 128), jnp.bfloat16)
    lane = lax.broadcasted_iota(jnp.int32, (1, 128), 1)
    for index in range(cells[0] * cells[1] * cells[2]):
        cx, cy, cz = index // (cells[1] * cells[2]), index // cells[2] % cells[1], index % cells[2]
        flat = total[index, 1:4].reshape(3 * 128, 128)
        high = flat.astype(jnp.bfloat16)
        middle = (flat - high.astype(jnp.float32)).astype(jnp.bfloat16)
        summed = sum(
            lax.dot_general(ones, piece, (((1,), (1,)), ((), ())), preferred_element_type=jnp.float32)[0:1]
            for piece in (high, middle)
        )
        across = [jnp.sum(jnp.transpose(total[index, k]), axis=0, keepdims=True) for k in (0, 4)]
        sums = [across[0]] + [summed[:, 128 * k : 128 * (k + 1)] for k in range(3)] + [across[1]]
        tile = halo_ref[cx + 1, cy + 1, cz + 1]
        live = lane < counts[cx + 1, cy + 1, cz + 1]
        place = sum(split2(tile[0:3] - 0.5))
        accel = [jnp.where(live, place[k : k + 1] * sums[0] - sums[k + 1], 0.0) for k in range(3)]
        accel[2] = accel[2] - GRAVITY
        visit(cx, cy, cz, accel, jnp.where(live, -sums[4], 0.0))


def scratch_for(halo_shape, cells):
    own = cells[0] * cells[1] * cells[2]
    slot = [pltpu.VMEM((2, 128, 256), jnp.float32), pltpu.VMEM((2, FIELDS, 128), jnp.float32)]
    return [
        pltpu.SMEM(halo_shape[:3], jnp.int32),
        pltpu.SMEM((own,), jnp.int32),
        pltpu.VMEM((own, 32, FIELDS, 128), jnp.float32),
        pltpu.VMEM((own, 5, 128, 128), jnp.float32),
        *slot,
        *slot,
    ]


PREPARE = pl.CostEstimate(flops=10**9, bytes_accessed=10**6, transcendentals=0)


def call(kernel, cells, outs, args, scratch=(), source=pltpu.VMEM, cost=None):
    whole = pl.BlockSpec(memory_space=pltpu.VMEM)
    return pl.pallas_call(
        functools.partial(kernel, cells),
        out_shape=[out if hasattr(out, "dtype") else jax.ShapeDtypeStruct(out, jnp.float32) for out in outs],
        in_specs=[pl.BlockSpec(memory_space=source)] * len(args),
        out_specs=[whole] * len(outs),
        scratch_shapes=list(scratch),
        cost_estimate=cost,
        compiler_params=pltpu.CompilerParams(vmem_limit_bytes=16 * 1024 * 1024),
    )(*args)


def all_cells(cells):
    return [(x, y, z) for x in range(cells[0]) for y in range(cells[1]) for z in range(cells[2])]


def state_kernel(cells, *refs):
    sources, (state_ref, target_ref), copies, arrived = refs[:7], refs[7:9], refs[9:16], refs[16]
    moves = [pltpu.make_async_copy(sources[k], copies[k], arrived.at[k]) for k in range(len(sources))]
    for move in moves:
        move.start()
    for move in moves:
        move.wait()
    offsets_ref, velocity_ref, density_ref, mass_ref, direction_ref, slot_ref, occupancy_ref = copies
    lane = lax.broadcasted_iota(jnp.int32, (1, 128), 1)
    for cx, cy, cz in all_cells(cells):
        here = pl.ds(cz, 1)
        for k in range(3):
            state_ref[cx, cy, cz, k : k + 1] = offsets_ref[k, cx, cy, here]
            state_ref[cx, cy, cz, k + 3 : k + 4] = velocity_ref[k, cx, cy, here]
        state_ref[cx, cy, cz, 6:7] = density_ref[cx, cy, here]
        live = lane < occupancy_ref[cx, cy, cz]
        state_ref[cx, cy, cz, 7:8] = jnp.where(live, mass_ref[cx, cy, here], 0.0)
        way, slot = direction_ref[cx, cy, here], slot_ref[cx, cy, here]
        target = jnp.where(way == 1, slot, jnp.where(way == 2, slot + MOVES, -1))
        target_ref[cx, cy, here] = jnp.where(live, target, -2)


def half_kernel(cells, halo_ref, own_ref, terms_ref, half_ref, *scratch):
    def visit(cx, cy, cz, accel, rate):
        tile = halo_ref[cx + 1, cy + 1, cz + 1]
        change = jnp.concatenate([tile[3:6]] + accel + [rate, jnp.zeros_like(rate)], 0)
        half_ref[cx, cy, cz] = tile + HALF_STEP * change

    over_cells(halo_ref, own_ref, terms_ref, scratch, cells, visit)


def last_kernel(cells, halo_ref, own_ref, terms_ref, state_ref, target_ref, lower_ref, upper_ref, kept_ref, *scratch):
    slots = lax.broadcasted_iota(jnp.int32, (2 * MOVES, 128), 0)
    row = lax.broadcasted_iota(jnp.int32, (FIELDS, 128), 0)
    lists = [jnp.zeros((FIELDS, 2 * MOVES), jnp.float32)]

    def visit(cx, cy, cz, accel, rate):
        tile = state_ref[cx, cy, cz]
        half = halo_ref[cx + 1, cy + 1, cz + 1]
        change = jnp.concatenate([half[3:6]] + accel + [rate, jnp.zeros_like(rate)], 0)
        new = tile + TIME_STEP * change
        target = target_ref[cx, cy, pl.ds(cz, 1)]
        kept_ref[cx, cy, cz] = jnp.where(target == -1, new, 0.0)
        chosen = (slots == target).astype(jnp.float32).astype(jnp.bfloat16)
        place = jnp.where(row == 0, float(cx), jnp.where(row == 1, float(cy), jnp.where(row == 2, float(cz), 0.0)))
        record = jnp.where(row == 7, 1.0, new + place)
        for piece in split3(record):
            lists[0] += lax.dot_general(
                piece.astype(jnp.bfloat16), chosen, (((1,), (1,)), ((), ())), preferred_element_type=jnp.float32
            )

    over_cells(halo_ref, own_ref, terms_ref, scratch, cells, visit)
    for side, (out_ref, moved) in enumerate(((lower_ref, -float(cells[0])), (upper_ref, float(cells[0])))):
        half = lists[0][:, MOVES * side : MOVES * (side + 1)]
        out_ref[...] = half + jnp.where(row == 0, moved, 0.0) * half[7:8]


def output_kernel(cells, kept_ref, position_ref, velocity_ref, density_ref):
    for cx, cy, cz in all_cells(cells):
        here = pl.ds(cz, 1)
        for k in range(3):
            position_ref[k, cx, cy, here] = kept_ref[cx, cy, cz, k : k + 1]
            velocity_ref[k, cx, cy, here] = kept_ref[cx, cy, cz, k + 3 : k + 4]
        density_ref[cx, cy, here] = kept_ref[cx, cy, cz, 6:7]


def body(offsets, velocity, density, mass, occupancy, move_direction, move_slot):
    cells = density.shape[:3]
    tiles = (*cells, FIELDS, 128)
    fields = (offsets, velocity, density, mass, move_direction, move_slot, occupancy)
    places = jax.ShapeDtypeStruct(density.shape, jnp.int32)
    fields = tuple(pltpu.with_memory_space_constraint(field, pltpu.HBM) for field in fields)
    staged = [pltpu.VMEM(field.shape, field.dtype) for field in fields[:-1]]
    staged += [pltpu.SMEM(occupancy.shape, occupancy.dtype), pltpu.SemaphoreType.DMA((len(fields),))]
    state, target = call(state_kernel, cells, [tiles, places], fields, staged, source=pltpu.HBM)
    own = cells[0] * cells[1] * cells[2]
    sides = [jax.ShapeDtypeStruct((own, 256, 128), jnp.bfloat16), (own, 2, 128, 128)]
    halo = with_halo(state)
    prepared = call(own_kernel, cells, sides, (state,), cost=PREPARE)
    scratch = scratch_for(halo.shape, cells)
    (half,) = call(half_kernel, cells, [tiles], (halo, *prepared), scratch)
    halo = with_halo(half)
    prepared = call(own_kernel, cells, sides, (half,), cost=PREPARE)
    arguments = (halo, *prepared, state, target)
    lower, upper, kept = call(last_kernel, cells, [(FIELDS, MOVES), (FIELDS, MOVES), tiles], arguments, scratch)
    shapes = [offsets.shape, velocity.shape, density.shape]
    count, at = lax.axis_size("gx"), lax.axis_index("gx")
    position_next, velocity_next, density_next = call(output_kernel, cells, shapes, (kept,), cost=PREPARE)
    if count > 1:
        lower = lax.ppermute(lower, "gx", [(i, (i + 1) % count) for i in range(count)])
        upper = lax.ppermute(upper, "gx", [(i, (i - 1) % count) for i in range(count)])
    lists = jnp.stack([jnp.where(at == 0, 0.0, lower), jnp.where(at == count - 1, 0.0, upper)], 1)
    arrivals = lists[:7].reshape(7, 2, 1, 1, 1, MOVES)
    return (position_next, velocity_next, density_next, arrivals)


def solution(mesh):
    placed = (
        P(None, "gx", "gy", "gz", None),
        P(None, "gx", "gy", "gz", None),
        P("gx", "gy", "gz", None),
        P("gx", "gy", "gz", None),
        P("gx", "gy", "gz"),
        P("gx", "gy", "gz", None),
        P("gx", "gy", "gz", None),
    )
    return jax.shard_map(
        body,
        mesh=mesh,
        in_specs=placed,
        out_specs=(
            P(None, "gx", "gy", "gz", None),
            P(None, "gx", "gy", "gz", None),
            P("gx", "gy", "gz", None),
            P(None, None, "gx", "gy", "gz", None),
        ),
        check_vma=False,
    )
```

```python
import functools
import math

import jax
import jax.numpy as jnp
from jax import lax
from jax.experimental import pallas as pl
from jax.experimental.pallas import tpu as pltpu
from jax.sharding import PartitionSpec as P


MOVES = 128

SMOOTH = 0.5
KERNEL_NORM = 21.0 / (16.0 * math.pi * SMOOTH**3)
GRADIENT = 5.0 * KERNEL_NORM / SMOOTH**2
SOUND_SPEED = 10.0
STIFFNESS = SOUND_SPEED**2 / 7.0
VISCOSITY = 0.1
GRAVITY = 1.0
TIME_STEP = 0.1
HALF_STEP = 0.05

FIELDS = 8
TINY = 1e-24
VISC_SCALE = 2.0 * VISCOSITY * SOUND_SPEED * SMOOTH
SOFTENING = 0.01 * SMOOTH * SMOOTH
REACH = 2.0 * SMOOTH


def exchange(tiles, axis, dim):
    count, length = lax.axis_size(axis), tiles.shape[dim]
    last = lax.slice_in_dim(tiles, length - 1, length, axis=dim)
    first = lax.slice_in_dim(tiles, 0, 1, axis=dim)
    at = lax.axis_index(axis)
    if count == 1:
        before = after = jnp.zeros_like(first)
    elif count == 2:
        got = lax.ppermute(jnp.where(at == 0, last, first), axis, [(0, 1), (1, 0)])
        before = jnp.where(at == 0, 0.0, got)
        after = jnp.where(at == 0, got, 0.0)
    else:
        before = lax.ppermute(last, axis, [(i, (i + 1) % count) for i in range(count)])
        after = lax.ppermute(first, axis, [(i, (i - 1) % count) for i in range(count)])
        before = jnp.where(at == 0, 0.0, before)
        after = jnp.where(at == count - 1, 0.0, after)
    return jnp.concatenate([before, tiles, after], axis=dim)


def with_halo(tiles):
    part = exchange(exchange(tiles, "gy", 1), "gz", 2)
    return part, exchange(part, "gx", 0)


def split3(values):
    high = values.astype(jnp.bfloat16).astype(jnp.float32)
    left = values - high
    middle = left.astype(jnp.bfloat16).astype(jnp.float32)
    return high, middle, left - middle


def split2(values):
    high = values.astype(jnp.bfloat16).astype(jnp.float32)
    return high, (values - high).astype(jnp.bfloat16).astype(jnp.float32)


def squares(tile):
    product = tile * tile
    mixed = tile[0:3] * tile[3:6]
    return product[0:1] + product[1:2] + product[2:3], mixed[0:1] + mixed[1:2] + mixed[2:3]


def near_side(high, middle):
    square, mixed = squares(high + middle)
    extra = jnp.concatenate([square, mixed] + [jnp.zeros_like(square)] * 6, 0)
    row = lax.broadcasted_iota(jnp.int32, extra.shape, 0)
    extra_high, extra_middle, extra_low = split3(extra)
    extra_high = jnp.where((row >= 2) & (row < 5), 1.0, extra_high)
    pieces = [high, middle, high, middle, extra_high, extra_middle, extra_low, jnp.zeros_like(high)]
    return jnp.concatenate(pieces, 0).astype(jnp.bfloat16)


DEPTH = 8 * FIELDS


def own_side(tile):
    high, middle = split2(tile)
    square, mixed = squares(high + middle)
    zero, one = jnp.zeros_like(square), jnp.ones_like(square)
    sides = []
    for order, value, marks in (
        (lambda t: jnp.concatenate([-2.0 * t[0:3]] + [zero] * 5, 0), square, [one, zero]),
        (lambda t: -jnp.concatenate([t[3:6], t[0:3], zero, zero], 0), mixed, [zero, one]),
    ):
        rest = jnp.concatenate(marks + [zero] * 6, 0)
        first = jnp.concatenate(marks + list(split3(value)) + [zero] * 3, 0)
        pieces = [order(high)] * 2 + [order(middle)] * 2 + [first, rest, rest]
        pieces += [jnp.zeros_like(tile)] * (16 - len(pieces))
        sides.append(jnp.transpose(jnp.concatenate(pieces, 0)))
    return jnp.concatenate(sides, 0).astype(jnp.bfloat16)


def pressure_rows(tile):
    rho, mass = tile[6:7], tile[7:8]
    safe = jnp.where(mass > 0, rho, 1.0)
    square = safe * safe
    return safe * (1.0 / VISC_SCALE), STIFFNESS * (square * square * square * safe - 1.0) / square


def count_cells(halo_ref, counts, first):
    for x in range(halo_ref.shape[0]):
        for y in range(halo_ref.shape[1]):
            live = (halo_ref[x, y, :, 7] > 0).astype(jnp.float32)
            column = jnp.sum(live, axis=1, keepdims=True).astype(jnp.int32)
            for z in range(halo_ref.shape[2]):
                counts[x + first, y, z] = column[z, 0]


def neighbours(cells, inner):
    return [
        [
            (x, y, z)
            for x in range(cx, cx + 3)
            for y in range(cy, cy + 3)
            for z in range(cz, cz + 3)
            if (1 <= x <= cells[0]) == inner
        ]
        for cx, cy, cz in all_cells(cells)
    ]


def compact(load, counts, near, cells, lists, starts):
    lane = lax.broadcasted_iota(jnp.int32, (FIELDS, 128), 1)
    row = lax.broadcasted_iota(jnp.int32, (FIELDS, 128), 0)
    at, shifts = list(starts), {}
    for step in range(max(len(entries) for entries in lists)):
        for c, own in enumerate(all_cells(cells)):
            if step >= len(lists[c]):
                continue
            place = lists[c][step]
            shift = tuple(place[k] - own[k] - 1.5 for k in range(3))
            if shift not in shifts:
                sx, sy, sz = shift
                shifts[shift] = jnp.where(row == 0, sx, jnp.where(row == 1, sy, jnp.where(row == 2, sz, 0.0)))
            block, inside = lax.shift_right_logical(at[c], 7), at[c] & 127
            rolled = pltpu.roll(load(place) + shifts[shift], inside, axis=1)
            pltpu.store(near.at[c, block], rolled, mask=lane >= inside)
            near[c, block + 1] = rolled
            at[c] = at[c] + counts[place]
    return at


def own_kernel(cells, tiles_ref, own_ref, terms_ref):
    row = lax.broadcasted_iota(jnp.int32, (FIELDS, 128), 0)
    for index, place in enumerate(all_cells(cells)):
        tile = tiles_ref[place] - jnp.where(row < 3, 0.5, 0.0)
        own_ref[index] = own_side(tile)
        columns = jnp.transpose(jnp.concatenate(list(pressure_rows(tile)) + [jnp.zeros((6, 128), jnp.float32)], 0))
        for k in range(2):
            terms_ref[index, k] = jnp.broadcast_to(columns[:, k : k + 1], (128, 128))


def pair_sums(counts, near, blocks, own, terms, slots, total, cell, index):
    cx, cy, cz = cell
    total[index] = jnp.zeros(total.shape[1:], jnp.float32)
    here = counts[cx + 1, cy + 1, cz + 1]
    chunks = lax.shift_right_logical(here + 15, 4)
    count = blocks[index]

    def run(rows):
        def products(block, slot):
            pairs, listed = slot
            sides = []
            for side in range(2):
                tile = near[index, 2 * block + side]
                high, middle = split2(tile)
                sides.append(near_side(high, middle))
                listed[side, 0:3] = high[0:3] + middle[0:3]
                for k, value in enumerate((*pressure_rows(tile), GRADIENT * tile[7:8])):
                    listed[side, 3 + k : 4 + k] = value
            right = jnp.concatenate(sides, 1)
            for k in range(2):
                pairs[k, 0:rows] = jnp.dot(own[index, pl.ds(128 * k, rows), 0:DEPTH], right, preferred_element_type=jnp.float32)

        def add(slot):
            pairs, listed = slot
            js = [[jnp.broadcast_to(listed[side, k : k + 1], (8, 128)) for k in range(6)] for side in range(2)]
            for part in range(rows // 8):
                at = pl.ds(8 * part, 8)
                qi, ai = terms[index, 0, at], terms[index, 1, at]
                sums = [total[index, k, at] for k in range(5)]
                for side, (xj, yj, zj, qj, aj, mj) in enumerate(js):
                    lanes = pl.ds(128 * side, 128)
                    dist_sq, along = jnp.maximum(pairs[0, at, lanes], TINY), pairs[1, at, lanes]
                    dist = dist_sq * lax.rsqrt(dist_sq)
                    fall = jnp.maximum(1.0 - (dist if REACH == 1.0 else dist * (1.0 / REACH)), 0.0)
                    weight = fall * fall * fall * mj
                    viscous = jnp.minimum(along, 0.0) / ((dist_sq + SOFTENING) * (qi + qj))
                    push = weight * (ai + aj - viscous)
                    sums[0] += push
                    sums[1] += push * xj
                    sums[2] += push * yj
                    sums[3] += push * zj
                    sums[4] += weight * along
                for k in range(5):
                    total[index, k, at] = sums[k]

        products(0, slots[0])

        def step(pair, carry):
            products(2 * pair + 1, slots[1])
            add(slots[0])
            products(2 * pair + 2, slots[0])
            add(slots[1])
            return carry

        lax.fori_loop(0, lax.shift_right_logical(count, 1), step, 0)
        pl.when((count & 1) == 1)(lambda: add(slots[0]))

    for rows in range(16, 129, 16):
        pl.when(chunks == rows // 16)(functools.partial(run, rows))


def sum_lists(counts, near, blocks, own, terms, slots, total, cells):
    def one(index, carry):
        cz = index % cells[2]
        cy = lax.div(index, cells[2]) % cells[1]
        cx = lax.div(index, cells[1] * cells[2])
        pair_sums(counts, near, blocks, own, terms, slots, total, (cx, cy, cz), index)
        return carry

    lax.fori_loop(0, cells[0] * cells[1] * cells[2], one, 0)


def inner_kernel(cells, part_ref, own, terms, total, left, *scratch):
    counts, blocks, near = scratch[:3]
    count_cells(part_ref, counts, 1)
    lists = neighbours(cells, True)
    starts = [jnp.int32(0)] * len(lists)
    at = compact(lambda place: part_ref[place[0] - 1, place[1], place[2]], counts, near, cells, lists, starts)
    for c in range(len(lists)):
        blocks[c] = lax.shift_right_logical(at[c], 8)
    sum_lists(counts, near, blocks, own, terms, (scratch[3:5], scratch[5:7]), total, cells)
    for c in range(len(lists)):
        for side in range(2):
            left[c, side] = near[c, 2 * blocks[c] + side]


def over_cells(halo_ref, own, terms, inner, left, scratch, cells, visit):
    counts, blocks, near, total = scratch[:4]
    count_cells(halo_ref, counts, 0)
    lists = neighbours(cells, False)
    starts = []
    for c, places in enumerate(neighbours(cells, True)):
        starts.append(sum(counts[place] for place in places) & 255)
        for side in range(2):
            near[c, side] = left[c, side]
    at = compact(lambda place: halo_ref[place], counts, near, cells, lists, starts)
    lanes = lax.broadcasted_iota(jnp.int32, (FIELDS, 128), 1)
    for c in range(len(lists)):
        block, inside = lax.shift_right_logical(at[c], 7), at[c] & 127
        zeros = jnp.zeros((FIELDS, 128), jnp.float32)
        pltpu.store(near.at[c, block], zeros, mask=lanes >= inside)
        near[c, block + 1] = zeros
        blocks[c] = lax.shift_right_logical(at[c] + 255, 8)
    sum_lists(counts, near, blocks, own, terms, (scratch[4:6], scratch[6:8]), total, cells)
    ones = jnp.ones((16, 128), jnp.bfloat16)
    lane = lax.broadcasted_iota(jnp.int32, (1, 128), 1)
    for index in range(cells[0] * cells[1] * cells[2]):
        cx, cy, cz = index // (cells[1] * cells[2]), index // cells[2] % cells[1], index % cells[2]
        flat = (inner[index, 1:4] + total[index, 1:4]).reshape(3 * 128, 128)
        high = flat.astype(jnp.bfloat16)
        middle = (flat - high.astype(jnp.float32)).astype(jnp.bfloat16)
        summed = sum(
            lax.dot_general(ones, piece, (((1,), (1,)), ((), ())), preferred_element_type=jnp.float32)[0:1]
            for piece in (high, middle)
        )
        across = [jnp.sum(jnp.transpose(inner[index, k] + total[index, k]), axis=0, keepdims=True) for k in (0, 4)]
        sums = [across[0]] + [summed[:, 128 * k : 128 * (k + 1)] for k in range(3)] + [across[1]]
        tile = halo_ref[cx + 1, cy + 1, cz + 1]
        live = lane < counts[cx + 1, cy + 1, cz + 1]
        place = sum(split2(tile[0:3] - 0.5))
        accel = [jnp.where(live, place[k : k + 1] * sums[0] - sums[k + 1], 0.0) for k in range(3)]
        accel[2] = accel[2] - GRAVITY
        visit(cx, cy, cz, accel, jnp.where(live, -sums[4], 0.0))


def scratch_for(cells, last):
    own = cells[0] * cells[1] * cells[2]
    slot = [pltpu.VMEM((2, 128, 256), jnp.float32), pltpu.VMEM((2, FIELDS, 128), jnp.float32)]
    total = [pltpu.VMEM((own, 5, 128, 128), jnp.float32)] if last else []
    return [
        pltpu.SMEM(tuple(size + 2 for size in cells), jnp.int32),
        pltpu.SMEM((own,), jnp.int32),
        pltpu.VMEM((own, 32, FIELDS, 128), jnp.float32),
        *total,
        *slot,
        *slot,
    ]


PREPARE = pl.CostEstimate(flops=10**9, bytes_accessed=10**6, transcendentals=0)


def call(kernel, cells, outs, args, scratch=(), source=pltpu.VMEM, cost=None):
    whole = pl.BlockSpec(memory_space=pltpu.VMEM)
    return pl.pallas_call(
        functools.partial(kernel, cells),
        out_shape=[out if hasattr(out, "dtype") else jax.ShapeDtypeStruct(out, jnp.float32) for out in outs],
        in_specs=[pl.BlockSpec(memory_space=source)] * len(args),
        out_specs=[whole] * len(outs),
        scratch_shapes=list(scratch),
        cost_estimate=cost,
        compiler_params=pltpu.CompilerParams(vmem_limit_bytes=16 * 1024 * 1024),
    )(*args)


def all_cells(cells):
    return [(x, y, z) for x in range(cells[0]) for y in range(cells[1]) for z in range(cells[2])]


def state_kernel(cells, *refs):
    sources, (state_ref, target_ref), copies, arrived = refs[:7], refs[7:9], refs[9:16], refs[16]
    moves = [pltpu.make_async_copy(sources[k], copies[k], arrived.at[k]) for k in range(len(sources))]
    for move in moves:
        move.start()
    for move in moves:
        move.wait()
    offsets_ref, velocity_ref, density_ref, mass_ref, direction_ref, slot_ref, occupancy_ref = copies
    lane = lax.broadcasted_iota(jnp.int32, (1, 128), 1)
    for cx, cy, cz in all_cells(cells):
        here = pl.ds(cz, 1)
        for k in range(3):
            state_ref[cx, cy, cz, k : k + 1] = offsets_ref[k, cx, cy, here]
            state_ref[cx, cy, cz, k + 3 : k + 4] = velocity_ref[k, cx, cy, here]
        state_ref[cx, cy, cz, 6:7] = density_ref[cx, cy, here]
        live = lane < occupancy_ref[cx, cy, cz]
        state_ref[cx, cy, cz, 7:8] = jnp.where(live, mass_ref[cx, cy, here], 0.0)
        way, slot = direction_ref[cx, cy, here], slot_ref[cx, cy, here]
        target = jnp.where(way == 1, slot, jnp.where(way == 2, slot + MOVES, -1))
        target_ref[cx, cy, here] = jnp.where(live, target, -2)


def half_kernel(cells, halo_ref, own_ref, terms_ref, inner_ref, left_ref, half_ref, *scratch):
    def visit(cx, cy, cz, accel, rate):
        tile = halo_ref[cx + 1, cy + 1, cz + 1]
        change = jnp.concatenate([tile[3:6]] + accel + [rate, jnp.zeros_like(rate)], 0)
        half_ref[cx, cy, cz] = tile + HALF_STEP * change

    over_cells(halo_ref, own_ref, terms_ref, inner_ref, left_ref, scratch, cells, visit)


def last_kernel(
    cells, halo_ref, own_ref, terms_ref, inner_ref, left_ref, state_ref, target_ref, lower_ref, upper_ref, kept_ref, *scratch
):
    slots = lax.broadcasted_iota(jnp.int32, (2 * MOVES, 128), 0)
    row = lax.broadcasted_iota(jnp.int32, (FIELDS, 128), 0)
    lists = [jnp.zeros((FIELDS, 2 * MOVES), jnp.float32)]

    def visit(cx, cy, cz, accel, rate):
        tile = state_ref[cx, cy, cz]
        half = halo_ref[cx + 1, cy + 1, cz + 1]
        change = jnp.concatenate([half[3:6]] + accel + [rate, jnp.zeros_like(rate)], 0)
        new = tile + TIME_STEP * change
        target = target_ref[cx, cy, pl.ds(cz, 1)]
        kept_ref[cx, cy, cz] = jnp.where(target == -1, new, 0.0)
        chosen = (slots == target).astype(jnp.float32).astype(jnp.bfloat16)
        place = jnp.where(row == 0, float(cx), jnp.where(row == 1, float(cy), jnp.where(row == 2, float(cz), 0.0)))
        record = jnp.where(row == 7, 1.0, new + place)
        for piece in split3(record):
            lists[0] += lax.dot_general(
                piece.astype(jnp.bfloat16), chosen, (((1,), (1,)), ((), ())), preferred_element_type=jnp.float32
            )

    over_cells(halo_ref, own_ref, terms_ref, inner_ref, left_ref, scratch, cells, visit)
    for side, (out_ref, moved) in enumerate(((lower_ref, -float(cells[0])), (upper_ref, float(cells[0])))):
        half = lists[0][:, MOVES * side : MOVES * (side + 1)]
        out_ref[...] = half + jnp.where(row == 0, moved, 0.0) * half[7:8]


def output_kernel(cells, kept_ref, position_ref, velocity_ref, density_ref):
    for cx, cy, cz in all_cells(cells):
        here = pl.ds(cz, 1)
        for k in range(3):
            position_ref[k, cx, cy, here] = kept_ref[cx, cy, cz, k : k + 1]
            velocity_ref[k, cx, cy, here] = kept_ref[cx, cy, cz, k + 3 : k + 4]
        density_ref[cx, cy, here] = kept_ref[cx, cy, cz, 6:7]


def body(offsets, velocity, density, mass, occupancy, move_direction, move_slot):
    cells = density.shape[:3]
    tiles = (*cells, FIELDS, 128)
    fields = (offsets, velocity, density, mass, move_direction, move_slot, occupancy)
    places = jax.ShapeDtypeStruct(density.shape, jnp.int32)
    fields = tuple(pltpu.with_memory_space_constraint(field, pltpu.HBM) for field in fields)
    staged = [pltpu.VMEM(field.shape, field.dtype) for field in fields[:-1]]
    staged += [pltpu.SMEM(occupancy.shape, occupancy.dtype), pltpu.SemaphoreType.DMA((len(fields),))]
    state, target = call(state_kernel, cells, [tiles, places], fields, staged, source=pltpu.HBM)
    own = cells[0] * cells[1] * cells[2]
    sides = [jax.ShapeDtypeStruct((own, 256, 128), jnp.bfloat16), (own, 2, 128, 128)]
    sums = [(own, 5, 128, 128), (own, 2, FIELDS, 128)]

    def gather(values):
        part, halo = with_halo(values)
        prepared = call(own_kernel, cells, sides, (values,), cost=PREPARE)
        inner = call(inner_kernel, cells, sums, (part, *prepared), scratch_for(cells, False), cost=PREPARE)
        return (halo, *prepared, *inner)

    scratch = scratch_for(cells, True)
    arguments = gather(state)
    (half,) = call(half_kernel, cells, [tiles], arguments, scratch)
    arguments = (*gather(half), state, target)
    lower, upper, kept = call(last_kernel, cells, [(FIELDS, MOVES), (FIELDS, MOVES), tiles], arguments, scratch)
    shapes = [offsets.shape, velocity.shape, density.shape]
    count, at = lax.axis_size("gx"), lax.axis_index("gx")
    position_next, velocity_next, density_next = call(output_kernel, cells, shapes, (kept,), cost=PREPARE)
    if count > 1:
        lower = lax.ppermute(lower, "gx", [(i, (i + 1) % count) for i in range(count)])
        upper = lax.ppermute(upper, "gx", [(i, (i - 1) % count) for i in range(count)])
    lists = jnp.stack([jnp.where(at == 0, 0.0, lower), jnp.where(at == count - 1, 0.0, upper)], 1)
    arrivals = lists[:7].reshape(7, 2, 1, 1, 1, MOVES)
    return (position_next, velocity_next, density_next, arrivals)


def solution(mesh):
    placed = (
        P(None, "gx", "gy", "gz", None),
        P(None, "gx", "gy", "gz", None),
        P("gx", "gy", "gz", None),
        P("gx", "gy", "gz", None),
        P("gx", "gy", "gz"),
        P("gx", "gy", "gz", None),
        P("gx", "gy", "gz", None),
    )
    return jax.shard_map(
        body,
        mesh=mesh,
        in_specs=placed,
        out_specs=(
            P(None, "gx", "gy", "gz", None),
            P(None, "gx", "gy", "gz", None),
            P("gx", "gy", "gz", None),
            P(None, None, "gx", "gy", "gz", None),
        ),
        check_vma=False,
    )
```

```python
import functools
import math

import jax
import jax.numpy as jnp
from jax import lax
from jax.experimental import pallas as pl
from jax.experimental.pallas import tpu as pltpu
from jax.sharding import PartitionSpec as P


MOVES = 128

SMOOTH = 0.5
KERNEL_NORM = 21.0 / (16.0 * math.pi * SMOOTH**3)
GRADIENT = 5.0 * KERNEL_NORM / SMOOTH**2
SOUND_SPEED = 10.0
STIFFNESS = SOUND_SPEED**2 / 7.0
VISCOSITY = 0.1
GRAVITY = 1.0
TIME_STEP = 0.1
HALF_STEP = 0.05

FIELDS = 8
TINY = 1e-24
VISC_SCALE = 2.0 * VISCOSITY * SOUND_SPEED * SMOOTH
SOFTENING = 0.01 * SMOOTH * SMOOTH
REACH = 2.0 * SMOOTH


def exchange(tiles, axis, dim):
    count, length = lax.axis_size(axis), tiles.shape[dim]
    last = lax.slice_in_dim(tiles, length - 1, length, axis=dim)
    first = lax.slice_in_dim(tiles, 0, 1, axis=dim)
    at = lax.axis_index(axis)
    if count == 1:
        before = after = jnp.zeros_like(first)
    elif count == 2:
        got = lax.ppermute(jnp.where(at == 0, last, first), axis, [(0, 1), (1, 0)])
        before = jnp.where(at == 0, 0.0, got)
        after = jnp.where(at == 0, got, 0.0)
    else:
        before = lax.ppermute(last, axis, [(i, (i + 1) % count) for i in range(count)])
        after = lax.ppermute(first, axis, [(i, (i - 1) % count) for i in range(count)])
        before = jnp.where(at == 0, 0.0, before)
        after = jnp.where(at == count - 1, 0.0, after)
    return jnp.concatenate([before, tiles, after], axis=dim)


def with_halo(tiles):
    first = exchange(tiles, "gy", 1)
    second = exchange(first, "gz", 2)
    return first, second, exchange(second, "gx", 0)


def split3(values):
    high = values.astype(jnp.bfloat16).astype(jnp.float32)
    left = values - high
    middle = left.astype(jnp.bfloat16).astype(jnp.float32)
    return high, middle, left - middle


def split2(values):
    high = values.astype(jnp.bfloat16).astype(jnp.float32)
    return high, (values - high).astype(jnp.bfloat16).astype(jnp.float32)


def squares(tile):
    product = tile * tile
    mixed = tile[0:3] * tile[3:6]
    return product[0:1] + product[1:2] + product[2:3], mixed[0:1] + mixed[1:2] + mixed[2:3]


def near_side(high, middle):
    square, mixed = squares(high + middle)
    extra = jnp.concatenate([square, mixed] + [jnp.zeros_like(square)] * 6, 0)
    row = lax.broadcasted_iota(jnp.int32, extra.shape, 0)
    extra_high, extra_middle, extra_low = split3(extra)
    extra_high = jnp.where((row >= 2) & (row < 5), 1.0, extra_high)
    pieces = [high, middle, high, middle, extra_high, extra_middle, extra_low, jnp.zeros_like(high)]
    return jnp.concatenate(pieces, 0).astype(jnp.bfloat16)


DEPTH = 8 * FIELDS


def own_side(tile):
    high, middle = split2(tile)
    square, mixed = squares(high + middle)
    zero, one = jnp.zeros_like(square), jnp.ones_like(square)
    sides = []
    for order, value, marks in (
        (lambda t: jnp.concatenate([-2.0 * t[0:3]] + [zero] * 5, 0), square, [one, zero]),
        (lambda t: -jnp.concatenate([t[3:6], t[0:3], zero, zero], 0), mixed, [zero, one]),
    ):
        rest = jnp.concatenate(marks + [zero] * 6, 0)
        first = jnp.concatenate(marks + list(split3(value)) + [zero] * 3, 0)
        pieces = [order(high)] * 2 + [order(middle)] * 2 + [first, rest, rest]
        pieces += [jnp.zeros_like(tile)] * (16 - len(pieces))
        sides.append(jnp.transpose(jnp.concatenate(pieces, 0)))
    return jnp.concatenate(sides, 0).astype(jnp.bfloat16)


def pressure_rows(tile):
    rho, mass = tile[6:7], tile[7:8]
    safe = jnp.where(mass > 0, rho, 1.0)
    square = safe * safe
    return safe * (1.0 / VISC_SCALE), STIFFNESS * (square * square * square * safe - 1.0) / square


def count_cells(tiles_ref, counts, x_first, z_first):
    for x in range(tiles_ref.shape[0]):
        for y in range(tiles_ref.shape[1]):
            live = (tiles_ref[x, y, :, 7] > 0).astype(jnp.float32)
            column = jnp.sum(live, axis=1, keepdims=True).astype(jnp.int32)
            for z in range(tiles_ref.shape[2]):
                counts[x + x_first, y, z + z_first] = column[z, 0]


def neighbours(cells, stage):
    return [
        [
            (x, y, z)
            for x in range(cx, cx + 3)
            for y in range(cy, cy + 3)
            for z in range(cz, cz + 3)
            if (2 if not 1 <= x <= cells[0] else 0 if 1 <= z <= cells[2] else 1) == stage
        ]
        for cx, cy, cz in all_cells(cells)
    ]


def starts_of(counts, cells, stage):
    earlier = [neighbours(cells, before) for before in range(stage)]
    return [
        sum((counts[place] for places in earlier for place in places[c]), jnp.int32(0)) & 255
        for c in range(cells[0] * cells[1] * cells[2])
    ]


def compact(load, counts, near, cells, lists, starts):
    lane = lax.broadcasted_iota(jnp.int32, (FIELDS, 128), 1)
    row = lax.broadcasted_iota(jnp.int32, (FIELDS, 128), 0)
    at, shifts = list(starts), {}
    for step in range(max(len(entries) for entries in lists)):
        for c, own in enumerate(all_cells(cells)):
            if step >= len(lists[c]):
                continue
            place = lists[c][step]
            shift = tuple(place[k] - own[k] - 1.5 for k in range(3))
            if shift not in shifts:
                sx, sy, sz = shift
                shifts[shift] = jnp.where(row == 0, sx, jnp.where(row == 1, sy, jnp.where(row == 2, sz, 0.0)))
            block, inside = lax.shift_right_logical(at[c], 7), at[c] & 127
            rolled = pltpu.roll(load(place) + shifts[shift], inside, axis=1)
            pltpu.store(near.at[c, block], rolled, mask=lane >= inside)
            near[c, block + 1] = rolled
            at[c] = at[c] + counts[place]
    return at


def own_kernel(cells, tiles_ref, own_ref, terms_ref):
    row = lax.broadcasted_iota(jnp.int32, (FIELDS, 128), 0)
    for index, place in enumerate(all_cells(cells)):
        tile = tiles_ref[place] - jnp.where(row < 3, 0.5, 0.0)
        own_ref[index] = own_side(tile)
        columns = jnp.transpose(jnp.concatenate(list(pressure_rows(tile)) + [jnp.zeros((6, 128), jnp.float32)], 0))
        for k in range(2):
            terms_ref[index, k] = jnp.broadcast_to(columns[:, k : k + 1], (128, 128))


def products(near, own, index, block, slot, rows):
    pairs, listed = slot
    sides = []
    for side in range(2):
        tile = near[index, 2 * block + side]
        high, middle = split2(tile)
        sides.append(near_side(high, middle))
        listed[side, 0:3] = high[0:3] + middle[0:3]
        for k, value in enumerate((*pressure_rows(tile), GRADIENT * tile[7:8])):
            listed[side, 3 + k : 4 + k] = value
    right = jnp.concatenate(sides, 1)
    for k in range(2):
        pairs[k, 0:rows] = jnp.dot(
            own[index, pl.ds(128 * k, rows), 0:DEPTH], right, preferred_element_type=jnp.float32
        )


def pair_sums(counts, near, blocks, own, terms, slots, total, cell, index):
    cx, cy, cz = cell
    here = counts[cx + 1, cy + 1, cz + 1]
    chunks = lax.shift_right_logical(here + 15, 4)
    count = blocks[index]

    def run(rows):
        def ahead(block, slot):
            products(near, own, index, block, slot, rows)

        def add(slot):
            pairs, listed = slot
            js = [[jnp.broadcast_to(listed[side, k : k + 1], (8, 128)) for k in range(6)] for side in range(2)]
            for part in range(rows // 8):
                at = pl.ds(8 * part, 8)
                qi, ai = terms[index, 0, at], terms[index, 1, at]
                sums = [total[index, k, at] for k in range(5)]
                for side, (xj, yj, zj, qj, aj, mj) in enumerate(js):
                    lanes = pl.ds(128 * side, 128)
                    dist_sq, along = jnp.maximum(pairs[0, at, lanes], TINY), pairs[1, at, lanes]
                    dist = dist_sq * lax.rsqrt(dist_sq)
                    fall = jnp.maximum(1.0 - (dist if REACH == 1.0 else dist * (1.0 / REACH)), 0.0)
                    weight = fall * fall * fall * mj
                    viscous = jnp.minimum(along, 0.0) / ((dist_sq + SOFTENING) * (qi + qj))
                    push = weight * (ai + aj - viscous)
                    sums[0] += push
                    sums[1] += push * xj
                    sums[2] += push * yj
                    sums[3] += push * zj
                    sums[4] += weight * along
                for k in range(5):
                    total[index, k, at] = sums[k]

        ahead(0, slots[0])

        def step(pair, carry):
            ahead(2 * pair + 1, slots[1])
            add(slots[0])
            ahead(2 * pair + 2, slots[0])
            add(slots[1])
            return carry

        lax.fori_loop(0, lax.shift_right_logical(count, 1), step, 0)
        pl.when((count & 1) == 1)(lambda: add(slots[0]))

    for rows in range(16, 129, 16):
        pl.when((chunks == rows // 16) & (count > 0))(functools.partial(run, rows))


def sum_lists(counts, near, blocks, own, terms, slots, total, cells):
    def one(index, carry):
        cz = index % cells[2]
        cy = lax.div(index, cells[2]) % cells[1]
        cx = lax.div(index, cells[1] * cells[2])
        pair_sums(counts, near, blocks, own, terms, slots, total, (cx, cy, cz), index)
        return carry

    lax.fori_loop(0, cells[0] * cells[1] * cells[2], one, 0)


def early_kernel(stage, cells, part_ref, own, terms, *refs):
    given, (total, left), scratch = refs[: 2 * stage], refs[2 * stage : 2 * stage + 2], refs[2 * stage + 2 :]
    counts, blocks, near = scratch[:3]
    z_first = 1 - stage
    count_cells(part_ref, counts, 1, z_first)
    lists = neighbours(cells, stage)
    if stage:
        total[...] = given[0][...]
        for c in range(len(lists)):
            for side in range(2):
                near[c, side] = given[1][c, side]
    else:
        total[...] = jnp.zeros(total.shape, jnp.float32)
    at = compact(
        lambda place: part_ref[place[0] - 1, place[1], place[2] - z_first],
        counts,
        near,
        cells,
        lists,
        starts_of(counts, cells, stage),
    )
    for c in range(len(lists)):
        blocks[c] = lax.shift_right_logical(at[c], 8)
    sum_lists(counts, near, blocks, own, terms, (scratch[3:5], scratch[5:7]), total, cells)
    for c in range(len(lists)):
        for side in range(2):
            left[c, side] = near[c, 2 * blocks[c] + side]


def over_cells(halo_ref, own, terms, inner, left, scratch, cells, visit):
    counts, blocks, near, total = scratch[:4]
    count_cells(halo_ref, counts, 0, 0)
    lists = neighbours(cells, 2)
    for c in range(len(lists)):
        for side in range(2):
            near[c, side] = left[c, side]
    at = compact(lambda place: halo_ref[place], counts, near, cells, lists, starts_of(counts, cells, 2))
    lanes = lax.broadcasted_iota(jnp.int32, (FIELDS, 128), 1)
    for c in range(len(lists)):
        block, inside = lax.shift_right_logical(at[c], 7), at[c] & 127
        zeros = jnp.zeros((FIELDS, 128), jnp.float32)
        pltpu.store(near.at[c, block], zeros, mask=lanes >= inside)
        near[c, block + 1] = zeros
        blocks[c] = lax.shift_right_logical(at[c] + 255, 8)
    total[...] = inner[...]
    sum_lists(counts, near, blocks, own, terms, (scratch[4:6], scratch[6:8]), total, cells)
    ones = jnp.ones((16, 128), jnp.bfloat16)
    lane = lax.broadcasted_iota(jnp.int32, (1, 128), 1)
    for index in range(cells[0] * cells[1] * cells[2]):
        cx, cy, cz = index // (cells[1] * cells[2]), index // cells[2] % cells[1], index % cells[2]
        flat = total[index, 1:4].reshape(3 * 128, 128)
        high = flat.astype(jnp.bfloat16)
        middle = (flat - high.astype(jnp.float32)).astype(jnp.bfloat16)
        summed = sum(
            lax.dot_general(ones, piece, (((1,), (1,)), ((), ())), preferred_element_type=jnp.float32)[0:1]
            for piece in (high, middle)
        )
        across = [jnp.sum(jnp.transpose(total[index, k]), axis=0, keepdims=True) for k in (0, 4)]
        sums = [across[0]] + [summed[:, 128 * k : 128 * (k + 1)] for k in range(3)] + [across[1]]
        tile = halo_ref[cx + 1, cy + 1, cz + 1]
        live = lane < counts[cx + 1, cy + 1, cz + 1]
        place = sum(split2(tile[0:3] - 0.5))
        accel = [jnp.where(live, place[k : k + 1] * sums[0] - sums[k + 1], 0.0) for k in range(3)]
        accel[2] = accel[2] - GRAVITY
        visit(cx, cy, cz, accel, jnp.where(live, -sums[4], 0.0))


def scratch_for(cells, last):
    own = cells[0] * cells[1] * cells[2]
    slot = [(2, 128, 256), (2, FIELDS, 128)]
    total = [pltpu.VMEM((own, 5, 128, 128), jnp.float32)] if last else []
    return [
        pltpu.SMEM(tuple(size + 2 for size in cells), jnp.int32),
        pltpu.SMEM((own,), jnp.int32),
        pltpu.VMEM((own, 32, FIELDS, 128), jnp.float32),
        *total,
        *[pltpu.VMEM(shape, jnp.float32) for shape in slot],
        *[pltpu.VMEM(shape, jnp.float32) for shape in slot],
    ]


PREPARE = pl.CostEstimate(flops=10**9, bytes_accessed=10**6, transcendentals=0)


def call(kernel, cells, outs, args, scratch=(), source=pltpu.VMEM, cost=None):
    whole = pl.BlockSpec(memory_space=pltpu.VMEM)
    return pl.pallas_call(
        functools.partial(kernel, cells),
        out_shape=[out if hasattr(out, "dtype") else jax.ShapeDtypeStruct(out, jnp.float32) for out in outs],
        in_specs=[pl.BlockSpec(memory_space=source)] * len(args),
        out_specs=[whole] * len(outs),
        scratch_shapes=list(scratch),
        cost_estimate=cost,
        compiler_params=pltpu.CompilerParams(vmem_limit_bytes=16 * 1024 * 1024),
    )(*args)


def all_cells(cells):
    return [(x, y, z) for x in range(cells[0]) for y in range(cells[1]) for z in range(cells[2])]


def state_kernel(cells, *refs):
    sources, (state_ref, target_ref), copies, arrived = refs[:7], refs[7:9], refs[9:16], refs[16]
    moves = [pltpu.make_async_copy(sources[k], copies[k], arrived.at[k]) for k in range(len(sources))]
    for move in moves:
        move.start()
    for move in moves:
        move.wait()
    offsets_ref, velocity_ref, density_ref, mass_ref, direction_ref, slot_ref, occupancy_ref = copies
    lane = lax.broadcasted_iota(jnp.int32, (1, 128), 1)
    for cx, cy, cz in all_cells(cells):
        here = pl.ds(cz, 1)
        for k in range(3):
            state_ref[cx, cy, cz, k : k + 1] = offsets_ref[k, cx, cy, here]
            state_ref[cx, cy, cz, k + 3 : k + 4] = velocity_ref[k, cx, cy, here]
        state_ref[cx, cy, cz, 6:7] = density_ref[cx, cy, here]
        live = lane < occupancy_ref[cx, cy, cz]
        state_ref[cx, cy, cz, 7:8] = jnp.where(live, mass_ref[cx, cy, here], 0.0)
        way, slot = direction_ref[cx, cy, here], slot_ref[cx, cy, here]
        target = jnp.where(way == 1, slot, jnp.where(way == 2, slot + MOVES, -1))
        target_ref[cx, cy, here] = jnp.where(live, target, -2)


def half_kernel(cells, halo_ref, own_ref, terms_ref, inner_ref, left_ref, half_ref, *scratch):
    def visit(cx, cy, cz, accel, rate):
        tile = halo_ref[cx + 1, cy + 1, cz + 1]
        change = jnp.concatenate([tile[3:6]] + accel + [rate, jnp.zeros_like(rate)], 0)
        half_ref[cx, cy, cz] = tile + HALF_STEP * change

    over_cells(halo_ref, own_ref, terms_ref, inner_ref, left_ref, scratch, cells, visit)


def choice_kernel(cells, target_ref, chosen_ref):
    slots = lax.broadcasted_iota(jnp.int32, (2 * MOVES, 128), 0)
    for index, (cx, cy, cz) in enumerate(all_cells(cells)):
        hit = slots == target_ref[cx, cy, pl.ds(cz, 1)]
        chosen_ref[index] = hit.astype(jnp.float32).astype(jnp.bfloat16)


def last_kernel(
    cells,
    halo_ref,
    own_ref,
    terms_ref,
    inner_ref,
    left_ref,
    state_ref,
    target_ref,
    chosen_ref,
    lower_ref,
    upper_ref,
    kept_ref,
    *scratch,
):
    row = lax.broadcasted_iota(jnp.int32, (FIELDS, 128), 0)
    packed = [jnp.zeros((4 * FIELDS, 2 * MOVES), jnp.float32)]
    places = all_cells(cells)

    def visit(cx, cy, cz, accel, rate):
        tile = state_ref[cx, cy, cz]
        half = halo_ref[cx + 1, cy + 1, cz + 1]
        change = jnp.concatenate([half[3:6]] + accel + [rate, jnp.zeros_like(rate)], 0)
        new = tile + TIME_STEP * change
        kept_ref[cx, cy, cz] = jnp.where(target_ref[cx, cy, pl.ds(cz, 1)] == -1, new, 0.0)
        place = jnp.where(row == 0, float(cx), jnp.where(row == 1, float(cy), jnp.where(row == 2, float(cz), 0.0)))
        pieces = split3(jnp.where(row == 7, 1.0, new + place))
        pieces = jnp.concatenate([*pieces, jnp.zeros_like(tile)], 0).astype(jnp.bfloat16)
        packed[0] += lax.dot_general(
            pieces, chosen_ref[places.index((cx, cy, cz))], (((1,), (1,)), ((), ())), preferred_element_type=jnp.float32
        )

    over_cells(halo_ref, own_ref, terms_ref, inner_ref, left_ref, scratch, cells, visit)
    lists = packed[0][0:FIELDS] + packed[0][FIELDS : 2 * FIELDS] + packed[0][2 * FIELDS : 3 * FIELDS]
    for side, (out_ref, moved) in enumerate(((lower_ref, -float(cells[0])), (upper_ref, float(cells[0])))):
        part = lists[:, MOVES * side : MOVES * (side + 1)]
        out_ref[...] = part + jnp.where(row == 0, moved, 0.0) * part[7:8]


def output_kernel(cells, kept_ref, position_ref, velocity_ref, density_ref):
    for cx, cy, cz in all_cells(cells):
        here = pl.ds(cz, 1)
        for k in range(3):
            position_ref[k, cx, cy, here] = kept_ref[cx, cy, cz, k : k + 1]
            velocity_ref[k, cx, cy, here] = kept_ref[cx, cy, cz, k + 3 : k + 4]
        density_ref[cx, cy, here] = kept_ref[cx, cy, cz, 6:7]


def body(offsets, velocity, density, mass, occupancy, move_direction, move_slot):
    cells = density.shape[:3]
    tiles = (*cells, FIELDS, 128)
    fields = (offsets, velocity, density, mass, move_direction, move_slot, occupancy)
    places = jax.ShapeDtypeStruct(density.shape, jnp.int32)
    fields = tuple(pltpu.with_memory_space_constraint(field, pltpu.HBM) for field in fields)
    staged = [pltpu.VMEM(field.shape, field.dtype) for field in fields[:-1]]
    staged += [pltpu.SMEM(occupancy.shape, occupancy.dtype), pltpu.SemaphoreType.DMA((len(fields),))]
    state, target = call(state_kernel, cells, [tiles, places], fields, staged, source=pltpu.HBM)
    own = cells[0] * cells[1] * cells[2]
    sides = [jax.ShapeDtypeStruct((own, 256, 128), jnp.bfloat16), (own, 2, 128, 128)]
    sums = [(own, 5, 128, 128), (own, 2, FIELDS, 128)]

    def gather(values):
        first, second, halo = with_halo(values)
        early = scratch_for(cells, False)
        prepared = call(own_kernel, cells, sides, (values,), cost=PREPARE)
        kernel = functools.partial(early_kernel, 0)
        sofar = call(kernel, cells, sums, (first, *prepared), early, cost=PREPARE)
        kernel = functools.partial(early_kernel, 1)
        sofar = call(kernel, cells, sums, (second, *prepared, *sofar), early, cost=PREPARE)
        return (halo, *prepared, *sofar)

    scratch = scratch_for(cells, True)
    arguments = gather(state)
    (chosen,) = call(
        choice_kernel, cells, [jax.ShapeDtypeStruct((own, 2 * MOVES, 128), jnp.bfloat16)], (target,), cost=PREPARE
    )
    (half,) = call(half_kernel, cells, [tiles], arguments, scratch)
    arguments = (*gather(half), state, target, chosen)
    lower, upper, kept = call(last_kernel, cells, [(FIELDS, MOVES), (FIELDS, MOVES), tiles], arguments, scratch)
    shapes = [offsets.shape, velocity.shape, density.shape]
    count, at = lax.axis_size("gx"), lax.axis_index("gx")
    position_next, velocity_next, density_next = call(output_kernel, cells, shapes, (kept,), cost=PREPARE)
    if count > 1:
        lower = lax.ppermute(lower, "gx", [(i, (i + 1) % count) for i in range(count)])
        upper = lax.ppermute(upper, "gx", [(i, (i - 1) % count) for i in range(count)])
    lists = jnp.stack([jnp.where(at == 0, 0.0, lower), jnp.where(at == count - 1, 0.0, upper)], 1)
    arrivals = lists[:7].reshape(7, 2, 1, 1, 1, MOVES)
    return (position_next, velocity_next, density_next, arrivals)


def solution(mesh):
    placed = (
        P(None, "gx", "gy", "gz", None),
        P(None, "gx", "gy", "gz", None),
        P("gx", "gy", "gz", None),
        P("gx", "gy", "gz", None),
        P("gx", "gy", "gz"),
        P("gx", "gy", "gz", None),
        P("gx", "gy", "gz", None),
    )
    return jax.shard_map(
        body,
        mesh=mesh,
        in_specs=placed,
        out_specs=(
            P(None, "gx", "gy", "gz", None),
            P(None, "gx", "gy", "gz", None),
            P("gx", "gy", "gz", None),
            P(None, None, "gx", "gy", "gz", None),
        ),
        check_vma=False,
    )
```

```python
import functools
import math

import jax
import jax.numpy as jnp
from jax import lax
from jax.experimental import pallas as pl
from jax.experimental.pallas import tpu as pltpu
from jax.sharding import PartitionSpec as P


MOVES = 128

SMOOTH = 0.5
KERNEL_NORM = 21.0 / (16.0 * math.pi * SMOOTH**3)
GRADIENT = 5.0 * KERNEL_NORM / SMOOTH**2
SOUND_SPEED = 10.0
STIFFNESS = SOUND_SPEED**2 / 7.0
VISCOSITY = 0.1
GRAVITY = 1.0
TIME_STEP = 0.1
HALF_STEP = 0.05

FIELDS = 8
TINY = 1e-24
VISC_SCALE = 2.0 * VISCOSITY * SOUND_SPEED * SMOOTH
SOFTENING = 0.01 * SMOOTH * SMOOTH
REACH = 2.0 * SMOOTH


def exchange(tiles, axis, dim):
    count, length = lax.axis_size(axis), tiles.shape[dim]
    last = lax.slice_in_dim(tiles, length - 1, length, axis=dim)
    first = lax.slice_in_dim(tiles, 0, 1, axis=dim)
    at = lax.axis_index(axis)
    if count == 1:
        before = after = jnp.zeros_like(first)
    elif count == 2:
        got = lax.ppermute(jnp.where(at == 0, last, first), axis, [(0, 1), (1, 0)])
        before = jnp.where(at == 0, 0.0, got)
        after = jnp.where(at == 0, got, 0.0)
    else:
        before = lax.ppermute(last, axis, [(i, (i + 1) % count) for i in range(count)])
        after = lax.ppermute(first, axis, [(i, (i - 1) % count) for i in range(count)])
        before = jnp.where(at == 0, 0.0, before)
        after = jnp.where(at == count - 1, 0.0, after)
    return jnp.concatenate([before, tiles, after], axis=dim)


def with_halo(tiles):
    part = exchange(exchange(tiles, "gy", 1), "gz", 2)
    return part, exchange(part, "gx", 0)


def split3(values):
    high = values.astype(jnp.bfloat16).astype(jnp.float32)
    left = values - high
    middle = left.astype(jnp.bfloat16).astype(jnp.float32)
    return high, middle, left - middle


def split2(values):
    high = values.astype(jnp.bfloat16).astype(jnp.float32)
    return high, (values - high).astype(jnp.bfloat16).astype(jnp.float32)


def squares(tile):
    product = tile * tile
    mixed = tile[0:3] * tile[3:6]
    return product[0:1] + product[1:2] + product[2:3], mixed[0:1] + mixed[1:2] + mixed[2:3]


def near_side(high, middle):
    square, mixed = squares(high + middle)
    extra = jnp.concatenate([square, mixed] + [jnp.zeros_like(square)] * 6, 0)
    row = lax.broadcasted_iota(jnp.int32, extra.shape, 0)
    extra_high, extra_middle, extra_low = split3(extra)
    extra_high = jnp.where((row >= 2) & (row < 5), 1.0, extra_high)
    pieces = [high, middle, high, middle, extra_high, extra_middle, extra_low, jnp.zeros_like(high)]
    return jnp.concatenate(pieces, 0).astype(jnp.bfloat16)


DEPTH = 8 * FIELDS


def own_side(tile):
    high, middle = split2(tile)
    square, mixed = squares(high + middle)
    zero, one = jnp.zeros_like(square), jnp.ones_like(square)
    sides = []
    for order, value, marks in (
        (lambda t: jnp.concatenate([-2.0 * t[0:3]] + [zero] * 5, 0), square, [one, zero]),
        (lambda t: -jnp.concatenate([t[3:6], t[0:3], zero, zero], 0), mixed, [zero, one]),
    ):
        rest = jnp.concatenate(marks + [zero] * 6, 0)
        first = jnp.concatenate(marks + list(split3(value)) + [zero] * 3, 0)
        pieces = [order(high)] * 2 + [order(middle)] * 2 + [first, rest, rest]
        pieces += [jnp.zeros_like(tile)] * (16 - len(pieces))
        sides.append(jnp.transpose(jnp.concatenate(pieces, 0)))
    return jnp.concatenate(sides, 0).astype(jnp.bfloat16)


def pressure_rows(tile):
    rho, mass = tile[6:7], tile[7:8]
    safe = jnp.where(mass > 0, rho, 1.0)
    square = safe * safe
    return safe * (1.0 / VISC_SCALE), STIFFNESS * (square * square * square * safe - 1.0) / square


def count_cells(halo_ref, counts, first):
    for x in range(halo_ref.shape[0]):
        for y in range(halo_ref.shape[1]):
            live = (halo_ref[x, y, :, 7] > 0).astype(jnp.float32)
            column = jnp.sum(live, axis=1, keepdims=True).astype(jnp.int32)
            for z in range(halo_ref.shape[2]):
                counts[x + first, y, z] = column[z, 0]


def neighbours(cells, inner):
    return [
        [
            (x, y, z)
            for x in range(cx, cx + 3)
            for y in range(cy, cy + 3)
            for z in range(cz, cz + 3)
            if (1 <= x <= cells[0]) == inner
        ]
        for cx, cy, cz in all_cells(cells)
    ]


def compact(load, counts, near, cells, lists, starts):
    lane = lax.broadcasted_iota(jnp.int32, (FIELDS, 128), 1)
    row = lax.broadcasted_iota(jnp.int32, (FIELDS, 128), 0)
    at, shifts = list(starts), {}
    for step in range(max(len(entries) for entries in lists)):
        for c, own in enumerate(all_cells(cells)):
            if step >= len(lists[c]):
                continue
            place = lists[c][step]
            shift = tuple(place[k] - own[k] - 1.5 for k in range(3))
            if shift not in shifts:
                sx, sy, sz = shift
                shifts[shift] = jnp.where(row == 0, sx, jnp.where(row == 1, sy, jnp.where(row == 2, sz, 0.0)))
            block, inside = lax.shift_right_logical(at[c], 7), at[c] & 127
            rolled = pltpu.roll(load(place) + shifts[shift], inside, axis=1)
            pltpu.store(near.at[c, block], rolled, mask=lane >= inside)
            near[c, block + 1] = rolled
            at[c] = at[c] + counts[place]
    return at


def own_kernel(cells, tiles_ref, own_ref, terms_ref):
    row = lax.broadcasted_iota(jnp.int32, (FIELDS, 128), 0)
    for index, place in enumerate(all_cells(cells)):
        tile = tiles_ref[place] - jnp.where(row < 3, 0.5, 0.0)
        own_ref[index] = own_side(tile)
        columns = jnp.transpose(jnp.concatenate(list(pressure_rows(tile)) + [jnp.zeros((6, 128), jnp.float32)], 0))
        for k in range(2):
            terms_ref[index, k] = jnp.broadcast_to(columns[:, k : k + 1], (128, 128))


def products(near, own, index, block, slot, rows):
    pairs, listed = slot
    sides = []
    for side in range(2):
        tile = near[index, 2 * block + side]
        high, middle = split2(tile)
        sides.append(near_side(high, middle))
        listed[side, 0:3] = high[0:3] + middle[0:3]
        for k, value in enumerate((*pressure_rows(tile), GRADIENT * tile[7:8])):
            listed[side, 3 + k : 4 + k] = value
    right = jnp.concatenate(sides, 1)
    for k in range(2):
        pairs[k, 0:rows] = jnp.dot(
            own[index, pl.ds(128 * k, rows), 0:DEPTH], right, preferred_element_type=jnp.float32
        )


def pair_sums(counts, near, blocks, own, terms, slots, total, cell, index):
    cx, cy, cz = cell
    here = counts[cx + 1, cy + 1, cz + 1]
    chunks = lax.shift_right_logical(here + 15, 4)
    count = blocks[index]

    def run(rows):
        def ahead(block, slot):
            products(near, own, index, block, slot, rows)

        def add(slot):
            pairs, listed = slot
            js = [[jnp.broadcast_to(listed[side, k : k + 1], (8, 128)) for k in range(6)] for side in range(2)]
            for part in range(rows // 8):
                at = pl.ds(8 * part, 8)
                qi, ai = terms[index, 0, at], terms[index, 1, at]
                sums = [total[index, k, at] for k in range(5)]
                for side, (xj, yj, zj, qj, aj, mj) in enumerate(js):
                    lanes = pl.ds(128 * side, 128)
                    dist_sq, along = jnp.maximum(pairs[0, at, lanes], TINY), pairs[1, at, lanes]
                    dist = dist_sq * lax.rsqrt(dist_sq)
                    fall = jnp.maximum(1.0 - (dist if REACH == 1.0 else dist * (1.0 / REACH)), 0.0)
                    weight = fall * fall * fall * mj
                    viscous = jnp.minimum(along, 0.0) / ((dist_sq + SOFTENING) * (qi + qj))
                    push = weight * (ai + aj - viscous)
                    sums[0] += push
                    sums[1] += push * xj
                    sums[2] += push * yj
                    sums[3] += push * zj
                    sums[4] += weight * along
                for k in range(5):
                    total[index, k, at] = sums[k]

        ahead(0, slots[0])

        def step(pair, carry):
            ahead(2 * pair + 1, slots[1])
            add(slots[0])
            ahead(2 * pair + 2, slots[0])
            add(slots[1])
            return carry

        lax.fori_loop(0, lax.shift_right_logical(count, 1), step, 0)
        pl.when((count & 1) == 1)(lambda: add(slots[0]))

    for rows in range(16, 129, 16):
        pl.when(chunks == rows // 16)(functools.partial(run, rows))


def sum_lists(counts, near, blocks, own, terms, slots, total, cells):
    def one(index, carry):
        cz = index % cells[2]
        cy = lax.div(index, cells[2]) % cells[1]
        cx = lax.div(index, cells[1] * cells[2])
        pair_sums(counts, near, blocks, own, terms, slots, total, (cx, cy, cz), index)
        return carry

    lax.fori_loop(0, cells[0] * cells[1] * cells[2], one, 0)


def inner_kernel(cells, part_ref, own, terms, total, left, *scratch):
    counts, blocks, near = scratch[:3]
    total[...] = jnp.zeros(total.shape, jnp.float32)
    count_cells(part_ref, counts, 1)
    lists = neighbours(cells, True)
    starts = [jnp.int32(0)] * len(lists)
    at = compact(lambda place: part_ref[place[0] - 1, place[1], place[2]], counts, near, cells, lists, starts)
    for c in range(len(lists)):
        blocks[c] = lax.shift_right_logical(at[c], 8)
    sum_lists(counts, near, blocks, own, terms, (scratch[3:5], scratch[5:7]), total, cells)
    for c in range(len(lists)):
        for side in range(2):
            left[c, side] = near[c, 2 * blocks[c] + side]


def over_cells(halo_ref, own, terms, inner, left, scratch, cells, visit):
    counts, blocks, near, total = scratch[:4]
    total[...] = inner[...]
    count_cells(halo_ref, counts, 0)
    lists = neighbours(cells, False)
    starts = []
    for c, places in enumerate(neighbours(cells, True)):
        starts.append(sum(counts[place] for place in places) & 255)
        for side in range(2):
            near[c, side] = left[c, side]
    at = compact(lambda place: halo_ref[place], counts, near, cells, lists, starts)
    lanes = lax.broadcasted_iota(jnp.int32, (FIELDS, 128), 1)
    for c in range(len(lists)):
        block, inside = lax.shift_right_logical(at[c], 7), at[c] & 127
        zeros = jnp.zeros((FIELDS, 128), jnp.float32)
        pltpu.store(near.at[c, block], zeros, mask=lanes >= inside)
        near[c, block + 1] = zeros
        blocks[c] = lax.shift_right_logical(at[c] + 255, 8)
    sum_lists(counts, near, blocks, own, terms, (scratch[4:6], scratch[6:8]), total, cells)
    ones = jnp.ones((16, 128), jnp.bfloat16)
    lane = lax.broadcasted_iota(jnp.int32, (1, 128), 1)
    for index in range(cells[0] * cells[1] * cells[2]):
        cx, cy, cz = index // (cells[1] * cells[2]), index // cells[2] % cells[1], index % cells[2]
        flat = total[index, 1:4].reshape(3 * 128, 128)
        high = flat.astype(jnp.bfloat16)
        middle = (flat - high.astype(jnp.float32)).astype(jnp.bfloat16)
        summed = sum(
            lax.dot_general(ones, piece, (((1,), (1,)), ((), ())), preferred_element_type=jnp.float32)[0:1]
            for piece in (high, middle)
        )
        across = [jnp.sum(jnp.transpose(total[index, k]), axis=0, keepdims=True) for k in (0, 4)]
        sums = [across[0]] + [summed[:, 128 * k : 128 * (k + 1)] for k in range(3)] + [across[1]]
        tile = halo_ref[cx + 1, cy + 1, cz + 1]
        live = lane < counts[cx + 1, cy + 1, cz + 1]
        place = sum(split2(tile[0:3] - 0.5))
        accel = [jnp.where(live, place[k : k + 1] * sums[0] - sums[k + 1], 0.0) for k in range(3)]
        accel[2] = accel[2] - GRAVITY
        visit(cx, cy, cz, accel, jnp.where(live, -sums[4], 0.0))


def scratch_for(cells, last):
    own = cells[0] * cells[1] * cells[2]
    slot = [(2, 128, 256), (2, FIELDS, 128)]
    total = [pltpu.VMEM((own, 5, 128, 128), jnp.float32)] if last else []
    return [
        pltpu.SMEM(tuple(size + 2 for size in cells), jnp.int32),
        pltpu.SMEM((own,), jnp.int32),
        pltpu.VMEM((own, 32, FIELDS, 128), jnp.float32),
        *total,
        *[pltpu.VMEM(shape, jnp.float32) for shape in slot],
        *[pltpu.VMEM(shape, jnp.float32) for shape in slot],
    ]


PREPARE = pl.CostEstimate(flops=10**9, bytes_accessed=10**6, transcendentals=0)


def call(kernel, cells, outs, args, scratch=(), source=pltpu.VMEM, cost=None):
    whole = pl.BlockSpec(memory_space=pltpu.VMEM)
    return pl.pallas_call(
        functools.partial(kernel, cells),
        out_shape=[out if hasattr(out, "dtype") else jax.ShapeDtypeStruct(out, jnp.float32) for out in outs],
        in_specs=[pl.BlockSpec(memory_space=source)] * len(args),
        out_specs=[whole] * len(outs),
        scratch_shapes=list(scratch),
        cost_estimate=cost,
        compiler_params=pltpu.CompilerParams(vmem_limit_bytes=16 * 1024 * 1024),
    )(*args)


def all_cells(cells):
    return [(x, y, z) for x in range(cells[0]) for y in range(cells[1]) for z in range(cells[2])]


def state_kernel(cells, *refs):
    sources, (state_ref, target_ref), copies, arrived = refs[:7], refs[7:9], refs[9:16], refs[16]
    moves = [pltpu.make_async_copy(sources[k], copies[k], arrived.at[k]) for k in range(len(sources))]
    for move in moves:
        move.start()
    for move in moves:
        move.wait()
    offsets_ref, velocity_ref, density_ref, mass_ref, direction_ref, slot_ref, occupancy_ref = copies
    lane = lax.broadcasted_iota(jnp.int32, (1, 128), 1)
    for cx, cy, cz in all_cells(cells):
        here = pl.ds(cz, 1)
        for k in range(3):
            state_ref[cx, cy, cz, k : k + 1] = offsets_ref[k, cx, cy, here]
            state_ref[cx, cy, cz, k + 3 : k + 4] = velocity_ref[k, cx, cy, here]
        state_ref[cx, cy, cz, 6:7] = density_ref[cx, cy, here]
        live = lane < occupancy_ref[cx, cy, cz]
        state_ref[cx, cy, cz, 7:8] = jnp.where(live, mass_ref[cx, cy, here], 0.0)
        way, slot = direction_ref[cx, cy, here], slot_ref[cx, cy, here]
        target = jnp.where(way == 1, slot, jnp.where(way == 2, slot + MOVES, -1))
        target_ref[cx, cy, here] = jnp.where(live, target, -2)


def half_kernel(cells, halo_ref, own_ref, terms_ref, inner_ref, left_ref, half_ref, *scratch):
    def visit(cx, cy, cz, accel, rate):
        tile = halo_ref[cx + 1, cy + 1, cz + 1]
        change = jnp.concatenate([tile[3:6]] + accel + [rate, jnp.zeros_like(rate)], 0)
        half_ref[cx, cy, cz] = tile + HALF_STEP * change

    over_cells(halo_ref, own_ref, terms_ref, inner_ref, left_ref, scratch, cells, visit)


def choice_kernel(cells, target_ref, chosen_ref):
    slots = lax.broadcasted_iota(jnp.int32, (2 * MOVES, 128), 0)
    for index, (cx, cy, cz) in enumerate(all_cells(cells)):
        hit = slots == target_ref[cx, cy, pl.ds(cz, 1)]
        chosen_ref[index] = hit.astype(jnp.float32).astype(jnp.bfloat16)


def last_kernel(
    cells,
    halo_ref,
    own_ref,
    terms_ref,
    inner_ref,
    left_ref,
    state_ref,
    target_ref,
    chosen_ref,
    lower_ref,
    upper_ref,
    kept_ref,
    *scratch,
):
    row = lax.broadcasted_iota(jnp.int32, (FIELDS, 128), 0)
    packed = [jnp.zeros((4 * FIELDS, 2 * MOVES), jnp.float32)]
    places = all_cells(cells)

    def visit(cx, cy, cz, accel, rate):
        tile = state_ref[cx, cy, cz]
        half = halo_ref[cx + 1, cy + 1, cz + 1]
        change = jnp.concatenate([half[3:6]] + accel + [rate, jnp.zeros_like(rate)], 0)
        new = tile + TIME_STEP * change
        kept_ref[cx, cy, cz] = jnp.where(target_ref[cx, cy, pl.ds(cz, 1)] == -1, new, 0.0)
        place = jnp.where(row == 0, float(cx), jnp.where(row == 1, float(cy), jnp.where(row == 2, float(cz), 0.0)))
        pieces = split3(jnp.where(row == 7, 1.0, new + place))
        pieces = jnp.concatenate([*pieces, jnp.zeros_like(tile)], 0).astype(jnp.bfloat16)
        packed[0] += lax.dot_general(
            pieces, chosen_ref[places.index((cx, cy, cz))], (((1,), (1,)), ((), ())), preferred_element_type=jnp.float32
        )

    over_cells(halo_ref, own_ref, terms_ref, inner_ref, left_ref, scratch, cells, visit)
    lists = packed[0][0:FIELDS] + packed[0][FIELDS : 2 * FIELDS] + packed[0][2 * FIELDS : 3 * FIELDS]
    for side, (out_ref, moved) in enumerate(((lower_ref, -float(cells[0])), (upper_ref, float(cells[0])))):
        part = lists[:, MOVES * side : MOVES * (side + 1)]
        out_ref[...] = part + jnp.where(row == 0, moved, 0.0) * part[7:8]


def output_kernel(cells, kept_ref, position_ref, velocity_ref, density_ref):
    for cx, cy, cz in all_cells(cells):
        here = pl.ds(cz, 1)
        for k in range(3):
            position_ref[k, cx, cy, here] = kept_ref[cx, cy, cz, k : k + 1]
            velocity_ref[k, cx, cy, here] = kept_ref[cx, cy, cz, k + 3 : k + 4]
        density_ref[cx, cy, here] = kept_ref[cx, cy, cz, 6:7]


def body(offsets, velocity, density, mass, occupancy, move_direction, move_slot):
    cells = density.shape[:3]
    tiles = (*cells, FIELDS, 128)
    fields = (offsets, velocity, density, mass, move_direction, move_slot, occupancy)
    places = jax.ShapeDtypeStruct(density.shape, jnp.int32)
    fields = tuple(pltpu.with_memory_space_constraint(field, pltpu.HBM) for field in fields)
    staged = [pltpu.VMEM(field.shape, field.dtype) for field in fields[:-1]]
    staged += [pltpu.SMEM(occupancy.shape, occupancy.dtype), pltpu.SemaphoreType.DMA((len(fields),))]
    state, target = call(state_kernel, cells, [tiles, places], fields, staged, source=pltpu.HBM)
    own = cells[0] * cells[1] * cells[2]
    sides = [jax.ShapeDtypeStruct((own, 256, 128), jnp.bfloat16), (own, 2, 128, 128)]
    sums = [(own, 5, 128, 128), (own, 2, FIELDS, 128)]

    def gather(values):
        part, halo = with_halo(values)
        prepared = call(own_kernel, cells, sides, (values,), cost=PREPARE)
        inner = call(inner_kernel, cells, sums, (part, *prepared), scratch_for(cells, False), cost=PREPARE)
        return (halo, *prepared, *inner)

    scratch = scratch_for(cells, True)
    arguments = gather(state)
    (chosen,) = call(
        choice_kernel, cells, [jax.ShapeDtypeStruct((own, 2 * MOVES, 128), jnp.bfloat16)], (target,), cost=PREPARE
    )
    (half,) = call(half_kernel, cells, [tiles], arguments, scratch)
    arguments = (*gather(half), state, target, chosen)
    lower, upper, kept = call(last_kernel, cells, [(FIELDS, MOVES), (FIELDS, MOVES), tiles], arguments, scratch)
    shapes = [offsets.shape, velocity.shape, density.shape]
    count, at = lax.axis_size("gx"), lax.axis_index("gx")
    position_next, velocity_next, density_next = call(output_kernel, cells, shapes, (kept,), cost=PREPARE)
    if count > 1:
        lower = lax.ppermute(lower, "gx", [(i, (i + 1) % count) for i in range(count)])
        upper = lax.ppermute(upper, "gx", [(i, (i - 1) % count) for i in range(count)])
    lists = jnp.stack([jnp.where(at == 0, 0.0, lower), jnp.where(at == count - 1, 0.0, upper)], 1)
    arrivals = lists[:7].reshape(7, 2, 1, 1, 1, MOVES)
    return (position_next, velocity_next, density_next, arrivals)


def solution(mesh):
    placed = (
        P(None, "gx", "gy", "gz", None),
        P(None, "gx", "gy", "gz", None),
        P("gx", "gy", "gz", None),
        P("gx", "gy", "gz", None),
        P("gx", "gy", "gz"),
        P("gx", "gy", "gz", None),
        P("gx", "gy", "gz", None),
    )
    return jax.shard_map(
        body,
        mesh=mesh,
        in_specs=placed,
        out_specs=(
            P(None, "gx", "gy", "gz", None),
            P(None, "gx", "gy", "gz", None),
            P("gx", "gy", "gz", None),
            P(None, None, "gx", "gy", "gz", None),
        ),
        check_vma=False,
    )
```
